32 devices in a mesh: blocks: 2 (over x), strip: 16 (over z, y, core).
Axes of the slice: x: 2, y: 2, z: 4, core: 2. Of those that a mesh axis runs over, the one named last changes fastest.
Arguments:
- estimate: float32 [128, 256, 256], P(('blocks', 'strip')), parts along dimension 0, may hold values from 0.5 to 2
- views_data: bfloat16 [8, 128, 256, 256], P(None, ('blocks', 'strip')), parts along dimension 1, may hold values from 0.02 to 30, as said below
- kernel_x: float32 [8, 9], replicated, may hold values from 0.1 to 1
- kernel_y: float32 [8, 5], replicated, may hold values from 0.1 to 1
- kernel_z: float32 [8, 9], replicated, may hold values from 0.1 to 1
Outputs:
- deconvolved: float32 [128, 256, 256], P(('blocks', 'strip')), parts along dimension 0
The draws below stay inside these ranges and needn't reach their ends.
There are 2 independent parts, one for each index of `blocks`. The reference program is written for one: setup_inputs(seed, part) draws one part's arguments, and reference() takes and returns one part's arrays. A program takes and returns all parts, laid end to end along the dimension named above; an argument that names none is the same for every part. Nothing has to cross between parts.
Inputs may be any that keep to these rules, and one draw needn't show every extreme that they name: `views_data`: positive recorded intensities of each view.
All inputs are finite; a program needn't handle non-finite values.
Results may differ from the reference program's by a relative error of at most 0.00067.
Values may be sent and summed in bfloat16 or wider, within the bound.
No kernel may reach another device: no remote copies, remote signals or barrier semaphores. Data moves between devices by JAX's collectives and lax.ppermute only.
A program may use at most 128 MiB of HBM per device.

```python
import math
import jax
import jax.numpy as jnp
from jax import lax

VIEWS = 8
X = 256
Z = 256
ITERS = 2
RX = 4
RY = 2
RZ = 4
NY = 64


def draw_views_data(key, part):
    keys = jax.random.split(jax.random.fold_in(key, 11), 3)
    shape = (VIEWS, NY, X, Z)
    base = jnp.exp(jax.random.uniform(keys[0], shape, jnp.float32, math.log(0.3), math.log(3.0)))
    gains = jnp.exp(jax.random.uniform(keys[1], (VIEWS,), jnp.float32, -0.7, 0.7))
    slopes = jax.random.uniform(keys[2], (VIEWS,), jnp.float32, -0.4, 1.5)
    ypos = jnp.arange(NY, dtype=jnp.float32) / NY
    trend = (1.0 + 4.0 * ypos)[None, :] * (1.0 + slopes[:, None] * ypos[None, :]) / 4.0
    values = base * gains[:, None, None, None] * trend[:, :, None, None]
    return values.astype(jnp.bfloat16)


def levels(own_key, shape, pieces, low, top_value):
    factor_of, own = 1.0, jax.random.fold_in(own_key, 6)
    for position, shards_of in pieces:
        steps = jnp.exp(jax.random.uniform(jax.random.fold_in(own, position), (shards_of,), jnp.float32, low / len(pieces), top_value / len(pieces)))
        factor_of = factor_of * jnp.repeat(steps, shape[position] // shards_of).reshape([-1 if axis == position else 1 for axis in range(len(shape))])
    return factor_of


def setup_inputs(seed: int = 0, part: int = 0) -> dict:
    key_list = jax.random.split(jax.random.key(seed), 6)
    own_keys = jax.random.split(jax.random.fold_in(key_list[5], part), 6)
    estimate = jnp.clip(jnp.exp(math.log(2.0) - 1.3862944 * jax.random.uniform(own_keys[0], (NY, X, Z), jnp.float32) ** levels(own_keys[0], (NY, X, Z), ((0, 16),), -0.2, 0.2)), 0.5, 2.0)
    views_data = draw_views_data(jax.random.fold_in(jax.random.fold_in(key_list[5], part), 71), part)
    kernel_x = jnp.clip(jnp.exp(jax.random.uniform(key_list[2], (VIEWS, 2 * RX + 1), jnp.float32, math.log(0.1), math.log(1.0))), 0.1, 1.0)
    kernel_y = jnp.clip(jnp.exp(jax.random.uniform(key_list[3], (VIEWS, 2 * RY + 1), jnp.float32, math.log(0.1), math.log(1.0))), 0.1, 1.0)
    kernel_z = jnp.clip(jnp.exp(jax.random.uniform(key_list[4], (VIEWS, 2 * RZ + 1), jnp.float32, math.log(0.1), math.log(1.0))), 0.1, 1.0)
    return {"estimate": estimate, "views_data": views_data, "kernel_x": kernel_x, "kernel_y": kernel_y, "kernel_z": kernel_z}


def rounded(value):
    return lax.optimization_barrier(value.astype(jnp.bfloat16)).astype(jnp.float32)


def shifted(field, kernel, along, radius, mirror):
    length = field.shape[along]
    widths = [(0, 0)] * field.ndim
    widths[along] = (radius, radius)
    padded = jnp.pad(field, widths)
    total = jnp.zeros(field.shape, jnp.float32)
    for offset in range(2 * radius + 1):
        start = 2 * radius - offset if mirror else offset
        piece = lax.slice_in_dim(padded, start, start + length, axis=along)
        total = total + kernel[offset] * piece
    return total


def blurring(field, prof_y, prof_x, prof_z, mirror):
    first = rounded(shifted(field, prof_y, 0, RY, mirror))
    second = rounded(shifted(first, prof_x, 1, RX, mirror))
    return shifted(second, prof_z, 2, RZ, mirror)


def reference(estimate, views_data, kernel_x, kernel_y, kernel_z):
    norm_y = kernel_y / jnp.sum(kernel_y, axis=1, keepdims=True)
    norm_x = rounded(kernel_x / jnp.sum(kernel_x, axis=1, keepdims=True))
    norm_z = rounded(kernel_z / jnp.sum(kernel_z, axis=1, keepdims=True))
    totals = jnp.stack([jnp.sum(views_data[view].astype(jnp.float32)) for view in range(VIEWS)])
    weights = jnp.sum(totals) / (VIEWS * totals)
    for step in range(ITERS):
        image = rounded(estimate)
        logsum = jnp.zeros(estimate.shape, jnp.float32)
        for view in range(VIEWS):
            blurred = blurring(image, norm_y[view], norm_x[view], norm_z[view], False)
            ratio = rounded(weights[view] * views_data[view].astype(jnp.float32) / blurred)
            correction = blurring(ratio, norm_y[view], norm_x[view], norm_z[view], True)
            logsum = logsum + jnp.log(correction)
        estimate = estimate * jnp.exp(logsum / VIEWS)
    return estimate
```

```python
import functools

import jax
import jax.numpy as jnp
from jax import lax
from jax.experimental import pallas as pl
from jax.experimental.pallas import tpu as pltpu
from jax.sharding import PartitionSpec as P

BF = jnp.bfloat16
F32 = jnp.float32
CHUNKS = (2, 2, 2, 2)


def split(count):
    sizes = list(CHUNKS) if sum(CHUNKS) == count else [1] * count
    return sizes


def dot(left, right):
    return jnp.dot(left, right, preferred_element_type=F32)


def call(body, grid, args, specs, outs, out_specs, scratch, name, aliases=None, flops=0, moved=0):
    spec = pltpu.PrefetchScalarGridSpec(
        num_scalar_prefetch=1, grid=grid, in_specs=specs, out_specs=out_specs, scratch_shapes=scratch
    )
    return pl.pallas_call(
        body,
        grid_spec=spec,
        out_shape=outs,
        input_output_aliases=aliases or {},
        compiler_params=pltpu.CompilerParams(dimension_semantics=("arbitrary",) * len(grid)),
        cost_estimate=pl.CostEstimate(flops=flops, bytes_accessed=moved, transcendentals=0),
        name=name,
    )(*args)


def orient(odd, estimate):
    own, nx, nz = estimate.shape

    def body(odd_ref, est_ref, out_ref):
        out_ref[...] = est_ref[...].astype(BF)

    return call(
        body,
        (own,),
        (odd, estimate),
        [pl.BlockSpec((1, nx, nz), lambda i, o: (o[0] * i + (1 - o[0]) * (own - 1 - i), 0, 0))],
        jax.ShapeDtypeStruct((own, nx, nz), BF),
        pl.BlockSpec((1, nx, nz), lambda i, o: (i, 0, 0)),
        [],
        "orient",
        moved=6 * estimate.size,
    )


def parcel(odd, views, sizes):
    count, own, nx, nz = views.shape
    half = own // 2
    starts = [sum(sizes[:i]) for i in range(len(sizes))]

    def body(odd_ref, v_ref, total_ref, a_ref, *b_refs):
        view = pl.program_id(0)
        is_odd = odd_ref[0]
        total = None
        for row in range(own):
            part = v_ref[0, row].astype(F32)
            part = jnp.sum(part, axis=0, keepdims=True)
            total = part if total is None else total + part
        total = jnp.sum(total, axis=1, keepdims=True)
        total_ref[pl.ds(view, 1), :] = jnp.broadcast_to(total, (1, 128))
        for q in range(half):
            a_ref[0, q] = v_ref[0, is_odd * q + (1 - is_odd) * (own - 1 - q)]
        for b_ref, start, size in zip(b_refs, starts, sizes):

            @pl.when((view >= start) & (view < start + size))
            def _():
                for q in range(half):
                    at = own - half + q
                    b_ref[0, q] = v_ref[0, is_odd * at + (1 - is_odd) * (own - 1 - at)]

    def chunk(start, size):
        return pl.BlockSpec(
            (1, half, nx, nz), lambda v, o: (jnp.minimum(jnp.maximum(v - start, 0), size - 1), 0, 0, 0)
        )

    outs = [jax.ShapeDtypeStruct((count, 128), F32), jax.ShapeDtypeStruct((count, half, nx, nz), BF)]
    out_specs = [pl.BlockSpec((count, 128), lambda v, o: (0, 0)), pl.BlockSpec((1, half, nx, nz), lambda v, o: (v, 0, 0, 0))]
    for start, size in zip(starts, sizes):
        outs.append(jax.ShapeDtypeStruct((size, half, nx, nz), BF))
        out_specs.append(chunk(start, size))
    return call(
        body,
        (count,),
        (odd, views),
        [pl.BlockSpec((1, own, nx, nz), lambda v, o: (v, 0, 0, 0))],
        outs,
        out_specs,
        [],
        "parcel",
        moved=4 * views.size,
    )


def stage(name, odd, env, start, size, forward, backward, last, into=None, carry=None, final=False):
    norm, log_gain, mats = env["norm"], env["log_gain"], env["mats"]
    views = env["views"]
    count, own, nx, nz = views.shape
    taps = norm.shape[1]
    ry = taps // 2
    half = own // 2
    low_out = backward[0] // half if backward else 0
    names, args, specs = [], [], []

    def add(key, value, spec):
        names.append(key)
        args.append(value)
        specs.append(spec)

    def whole(value):
        return pl.BlockSpec(value.shape, lambda v, o: (0,) * value.ndim)

    add("norm", norm, pl.BlockSpec(memory_space=pltpu.SMEM))
    if final:
        add("gain", log_gain, pl.BlockSpec(memory_space=pltpu.SMEM))
    mat = pl.BlockSpec((1, nx, nx), lambda v, o: (start + v, 0, 0))
    for key in ("xf", "zf", "xb", "zb"):
        if key[1] == "f" or backward:
            add(key, mats[key], mat)
    need = set()
    for p in forward:
        for t in range(taps):
            need.add(locate_image(p + t - ry, own, half)[0])
    for key in sorted(need):
        value, block = env["image"][key]
        add("image_" + key, value, pl.BlockSpec((half, nx, nz), lambda v, o, block=block: (block, 0, 0)))
    need = {locate_data(p, own, half)[0] for p in forward}
    if "par" in need:
        add("data_par", env["data_par"], pl.BlockSpec((1, half, nx, nz), lambda v, o: (start + v, 0, 0, 0)))
    if "a" in need:
        add("data_a", views, pl.BlockSpec((1, half, nx, nz), lambda v, o: (start + v, 1 - o[0], 0, 0)))
    if "b" in need:
        add("data_b", views, pl.BlockSpec((1, half, nx, nz), lambda v, o: (start + v, o[0], 0, 0)))
    if "out" in need:
        add("data_out", env["data_out"], pl.BlockSpec((1, half, nx, nz), lambda v, o: (v, 0, 0, 0)))
    pairs_new = sorted({(p + ry) // half for p in forward})
    pairs_need = sorted({(y + t) // half for y in backward for t in range(taps)})
    for k in pairs_need:
        if k not in pairs_new:
            value, block = env["ratio"][k]
            add(f"ratio_{k}", value, pl.BlockSpec((1, half, nx, nz), lambda v, o, block=block: (start + v, block, 0, 0)))
    if backward and last:
        add("est", env["est"][low_out][0], env["est"][low_out][1])
    if carry is not None:
        add("carry", carry, whole(carry))
    aliases = {}
    if into is not None:
        aliases[len(args) + 1] = 0
        add("into", into, pl.BlockSpec(memory_space=pl.ANY))

    outs, out_specs, out_names = [], [], []

    def give(key, shape, dtype, spec):
        outs.append(jax.ShapeDtypeStruct(shape, dtype))
        out_specs.append(spec)
        out_names.append(key)

    part = pl.BlockSpec((half, nx, nz), lambda v, o: (0, 0, 0))
    if backward:
        if not last:
            give("sum", (half, nx, nz), F32, part)
        elif final:
            if low_out == 0:
                give("done", (own, nx, nz), F32, pl.BlockSpec((half, nx, nz), lambda v, o: (1 - o[0], 0, 0)))
            else:
                give("done", (own, nx, nz), F32, pl.BlockSpec((half, nx, nz), lambda v, o: (o[0], 0, 0)))
        else:
            give("est_new", (half, nx, nz), F32, part)
            give("image_new", (half, nx, nz), BF, part)
    store = env["store"]
    if store:
        give("ratio_new", (count, half * len(pairs_new), nx, nz), BF, pl.BlockSpec((1, half * len(pairs_new), nx, nz), lambda v, o: (v, 0, 0, 0)))
    scratch = [] if store else [pltpu.VMEM((1, half * len(pairs_new), nx, nz), BF)]
    if backward and last:
        scratch.append(pltpu.VMEM((half, nx, nz), F32))

    def body(odd_ref, *refs):
        ref = dict(zip(names, refs))
        out = dict(zip(out_names, refs[len(names) :]))
        rest = refs[len(names) + len(out_names) :]
        new = out["ratio_new"] if store else rest[0]
        total = out["sum"] if (backward and not last) else (rest[-1] if backward else None)
        view = pl.program_id(0)
        is_odd = odd_ref[0]

        def tap(t):
            return ref["norm"][start + view, is_odd * t + (1 - is_odd) * (taps - 1 - t)]

        weights = [tap(t) for t in range(taps)]

        def combine(rows):
            acc = None
            for t, row in enumerate(rows):
                term = weights[t] * row.astype(F32)
                acc = term if acc is None else acc + term
            return acc.astype(BF)

        def image(p):
            key, q = locate_image(p, own, half)
            return ref["image_" + key][q]

        def data(p):
            key, q = locate_data(p, own, half)
            if key in ("a", "b"):
                return ref["data_" + key][0, is_odd * q + (1 - is_odd) * (half - 1 - q)]
            return ref["data_" + key][0, q]

        def ratio(p):
            k, q = (p + ry) // half, (p + ry) % half
            if k in pairs_new:
                return new[0, half * pairs_new.index(k) + q]
            return ref[f"ratio_{k}"][0, q]

        xf, zf = ref["xf"][0], ref["zf"][0]
        for p in forward:
            first = combine([image(p + t - ry) for t in range(taps)])
            second = dot(xf, first).astype(BF)
            blurred = dot(second, zf)
            k, q = (p + ry) // half, (p + ry) % half
            new[0, half * pairs_new.index(k) + q] = (data(p).astype(F32) / blurred).astype(BF)
        if not backward:
            return
        xb, zb = ref["xb"][0], ref["zb"][0]

        @pl.when(view == 0)
        def _():
            total[...] = ref["carry"][...] if carry is not None else jnp.zeros_like(total)

        for i, y in enumerate(backward):
            first = combine([ratio(y + (taps - 1 - t) - ry) for t in range(taps)])
            second = dot(xb, first).astype(BF)
            total[i] += jnp.log(dot(second, zb))
        if not last:
            return

        @pl.when(view == size - 1)
        def _():
            for i in range(half):
                at = is_odd * i + (1 - is_odd) * (half - 1 - i)
                value = total[i] / count
                if final:
                    value = value + ref["gain"][0]
                if env["est_oriented"]:
                    out["done"][at] = ref["est"][i] * jnp.exp(value)
                else:
                    fresh = ref["est"][at] * jnp.exp(value)
                    if final:
                        out["done"][at] = fresh
                    else:
                        out["est_new"][i] = fresh
                        out["image_new"][i] = fresh.astype(BF)

    work = 2 * nx * nz * nx * 2 * size * (len(forward) + len(backward))
    got = call(body, (size,), [odd, *args], specs, outs, out_specs, scratch, name, aliases, flops=work, moved=2 * nx * nz * size * 12)
    return dict(zip(out_names, got))


def locate_image(p, own, half):
    if p < 0:
        key, q = "par", -1 - p
    elif p >= own:
        key, q = "out", 2 * own - 1 - p
    else:
        key, q = "own", p
    return key + "_" + ("a" if q < half else "b"), q % half


def locate_data(p, own, half):
    if p < 0:
        return "par", -1 - p
    if p >= own:
        return "out", 2 * own - 1 - p - half
    return ("a", p) if p < half else ("b", p - half)


def banded(kernel, length, flip):
    radius = kernel.shape[1] // 2
    rows = lax.broadcasted_iota(jnp.int32, (length, length), 0)
    columns = lax.broadcasted_iota(jnp.int32, (length, length), 1)
    grid = (columns - rows if flip else rows - columns) + radius
    matrix = jnp.zeros((kernel.shape[0], length, length), F32)
    for offset in range(2 * radius + 1):
        matrix = jnp.where((grid == offset)[None], kernel[:, offset][:, None, None], matrix)
    return matrix.astype(BF)


def summed(value, axis):
    count = lax.axis_size(axis)
    if count & (count - 1):
        return lax.psum(value, axis)
    step = 1
    while step < count:
        value = value + lax.ppermute(value, axis, [(i, i ^ step) for i in range(count)])
        step *= 2
    return value


def local(estimate, views_data, kernel_x, kernel_y, kernel_z):
    count = views_data.shape[0]
    own, nx, nz = estimate.shape
    half = own // 2
    ry = kernel_y.shape[1] // 2
    strip = lax.axis_size("strip")
    odd = (lax.axis_index("strip") % 2).astype(jnp.int32).reshape(1)
    pair = [(i, i ^ 1) for i in range(strip) if (i ^ 1) < strip]
    outer = []
    for i in range(1, strip - 1, 2):
        outer += [(i, i + 1), (i + 1, i)]

    def to_pair(x):
        return lax.ppermute(x, "strip", pair)

    def to_outer(x):
        return lax.ppermute(x, "strip", outer)

    sizes = split(count)
    image = orient(odd, estimate)
    image_par = to_pair(image)
    image_out = to_outer(image)
    totals, send_a, *send_b = parcel(odd, views_data, sizes)
    data_par = to_pair(send_a)
    data_out = [to_outer(b) for b in send_b]
    totals = summed(totals[:, 0], "strip")
    weights = jnp.sum(totals) / (count * totals)
    log_gain = (jnp.sum(jnp.log(weights)) / count).reshape(1)

    norm = kernel_y / jnp.sum(kernel_y, axis=1, keepdims=True)
    px = kernel_x / jnp.sum(kernel_x, axis=1, keepdims=True)
    pz = kernel_z / jnp.sum(kernel_z, axis=1, keepdims=True)
    mats = {
        "xf": banded(px, nx, True),
        "xb": banded(px, nx, False),
        "zf": banded(pz, nz, False),
        "zb": banded(pz, nz, True),
    }
    env = {
        "norm": norm,
        "log_gain": log_gain,
        "mats": mats,
        "views": views_data,
        "data_par": data_par,
        "image": {
            "par_a": (image_par, 0),
            "par_b": (image_par, 1),
            "own_a": (image, 0),
            "own_b": (image, 1),
            "out_a": (image_out, 0),
            "out_b": (image_out, 1),
        },
        "est": [
            (estimate, pl.BlockSpec((half, nx, nz), lambda v, o: (1 - o[0], 0, 0))),
            (estimate, pl.BlockSpec((half, nx, nz), lambda v, o: (o[0], 0, 0))),
        ],
        "est_oriented": False,
        "store": True,
    }
    got = stage("inner", odd, env, 0, count, (-2, -1, 0, 1, 2, 3), (0, 1), True)
    est_a, image_a = got["est_new"], got["image_new"]
    env["ratio"] = {k: (got["ratio_new"], k) for k in range(3)}
    env["store"] = False
    carry, start = None, 0
    for data, size in zip(data_out, sizes):
        env["data_out"] = data
        last = start + size == count
        got = stage("outer", odd, env, start, size, (4, 5), (2, 3), last, carry=carry)
        carry = None if last else got["sum"]
        start += size
    est_b, image_b = got["est_new"], got["image_new"]
    whole_out = jnp.concatenate(data_out, axis=0) if len(data_out) > 1 else data_out[0]

    par_a, par_b = to_pair(image_a), to_pair(image_b)
    out_b = to_outer(image_b)
    held, out_b_seen = lax.optimization_barrier((image_a, image_b))
    out_a = to_outer(held)
    part = pl.BlockSpec((half, nx, nz), lambda v, o: (0, 0, 0))
    env.update(
        image={
            "par_a": (par_a, 0),
            "par_b": (par_b, 0),
            "own_a": (image_a, 0),
            "own_b": (image_b, 0),
            "out_a": (out_a, 0),
            "out_b": (out_b, 0),
        },
        est=[(est_a, part), (est_b, part)],
        est_oriented=True,
        data_out=whole_out,
    )
    env["store"] = True
    got = stage("near", odd, env, 0, count, (-2, -1, 0, 1), (), False)
    env["ratio"] = {k: (got["ratio_new"], k) for k in range(2)}
    got = stage("middle", odd, env, 0, count, (2, 3), (0, 1), True, final=True)
    env["ratio"][2] = (got["ratio_new"], 0)
    env["store"] = False
    done = got["done"]
    got = stage("far", odd, env, 0, count, (4, 5), (2, 3), True, into=done, final=True)
    return got["done"]


def solution(mesh):
    placed = (
        P(("blocks", "strip"), None, None),
        P(None, ("blocks", "strip"), None, None),
        P(),
        P(),
        P(),
    )
    return jax.shard_map(
        local,
        mesh=mesh,
        in_specs=placed,
        out_specs=P(("blocks", "strip"), None, None),
        check_vma=False,
    )
```

```python
import jax
import jax.numpy as jnp
from jax import lax
from jax.experimental import pallas as pl
from jax.experimental.pallas import tpu as pltpu
from jax.sharding import PartitionSpec as P

BF = jnp.bfloat16
F32 = jnp.float32
CHUNKS = (5, 3)
GRANT = 24 * 1024 * 1024


def dot(left, right):
    return jnp.dot(left, right, preferred_element_type=F32)


def call(body, refs, outs, scratch, name, work=0):
    spaces = {"vmem": pltpu.VMEM, "smem": pltpu.SMEM, "any": pl.ANY}
    specs = [pl.BlockSpec(memory_space=spaces[where]) for _, where in refs.values()]
    moved = sum(value.size * value.dtype.itemsize for value, _ in refs.values())

    def kernel(*given):
        names = list(refs) + list(outs)
        body(dict(zip(names, given)), given[len(names) :])

    got = pl.pallas_call(
        kernel,
        in_specs=specs,
        out_specs=[pl.BlockSpec(memory_space=pltpu.VMEM) for _ in outs],
        out_shape=[jax.ShapeDtypeStruct(shape, dtype) for shape, dtype in outs.values()],
        scratch_shapes=scratch,
        compiler_params=pltpu.CompilerParams(vmem_limit_bytes=GRANT),
        cost_estimate=pl.CostEstimate(flops=work, bytes_accessed=moved, transcendentals=0),
        name=name,
    )(*[value for value, _ in refs.values()])
    return dict(zip(outs, got))


def orient(odd, estimate):
    own, nx, nz = estimate.shape

    def body(ref, scratch):
        is_odd = ref["odd"][0]
        for q in range(own):
            ref["image"][q] = ref["est"][is_odd * q + (1 - is_odd) * (own - 1 - q)].astype(BF)

    refs = {"odd": (odd, "smem"), "est": (estimate, "vmem")}
    return call(body, refs, {"image": ((own, nx, nz), BF)}, [], "orient")["image"]


def parcel(odd, views, sizes):
    count, own, nx, nz = views.shape
    half = own // 2
    outs = {"a": ((count, half, nx, nz), BF)}
    outs.update({f"b{i}": ((size, half, nx, nz), BF) for i, size in enumerate(sizes)})

    def body(ref, scratch):
        is_odd = ref["odd"][0]
        sems = scratch[0]
        near, far = (1 - is_odd) * half, is_odd * half
        copies = []
        at = 0
        for i, size in enumerate(sizes):
            source = ref["views"].at[pl.ds(at, size), pl.ds(far, half)]
            copies.append(pltpu.make_async_copy(source, ref[f"b{i}"], sems.at[i]))
            at += size
        source = ref["views"].at[:, pl.ds(near, half)]
        copies.append(pltpu.make_async_copy(source, ref["a"], sems.at[len(sizes)]))
        for copy in copies:
            copy.start()
        for copy in copies:
            copy.wait()

    refs = {"odd": (odd, "smem"), "views": (views, "any")}
    got = call(body, refs, outs, [pltpu.SemaphoreType.DMA((len(sizes) + 1,))], "parcel")
    return got["a"], [got[f"b{i}"] for i in range(len(sizes))]


def sums(views):
    count, own, nx, nz = views.shape

    def body(ref, scratch):
        def step(view, _):
            total = jnp.zeros((8, nz), F32)
            for row in range(own):
                part = ref["views"][view, row].astype(F32)
                total = total + jnp.sum(part.reshape(nx // 8, 8, nz), axis=0)
            total = jnp.sum(jnp.sum(total, axis=0, keepdims=True), axis=1, keepdims=True)
            ref["total"][pl.ds(view, 1), :] = jnp.broadcast_to(total, (1, 128))
            return 0

        lax.fori_loop(0, count, step, 0)

    return call(body, {"views": (views, "vmem")}, {"total": ((count, 128), F32)}, [], "sums")["total"]


def locate_image(p, own, half):
    if p < 0:
        key, q = "par", -1 - p
    elif p >= own:
        key, q = "out", 2 * own - 1 - p
    else:
        key, q = "own", p
    return key, q


def stage(name, env, chunks, forward, backward, last=True, carry=None, store=False, final=False):
    views, norm, mats = env["views"], env["norm"], env["mats"]
    count, own, nx, nz = views.shape
    taps = norm.shape[1]
    ry = taps // 2
    half = own // 2
    refs = {"odd": (env["odd"], "smem"), "norm": (norm, "smem")}
    for key in ("xf", "zf") + (("xb", "zb") if backward else ()):
        refs[key] = (mats[key], "vmem")
    reach = {locate_image(p + t - ry, own, half) for p in forward for t in range(taps)}
    for key, q in sorted(reach):
        value = env["image"][key][q // half]
        refs[f"image_{key}{q // half}"] = (value, "vmem")
    if any(p < 0 for p in forward):
        refs["data_par"] = (env["data_par"], "vmem")
    if any(0 <= p < own for p in forward):
        refs["views"] = (views, "vmem")
    for i, (_, _, data) in enumerate(chunks):
        if data is not None:
            refs[f"data_out{i}"] = (data, "vmem")
    new = [p + ry for p in forward]
    old = sorted({y + t for y in backward for t in range(taps)} - set(new))
    for at in old:
        value, _ = env["ratio"][at]
        key = "ratio%d" % [id(v) for v in env["held"]].index(id(value))
        refs[key] = (value, "vmem")
    low_out = backward[0] if backward else 0
    if backward and last:
        refs["est"] = (env["est"], "vmem")
    if carry is not None:
        refs["carry"] = (carry, "vmem")
    if final:
        refs["gain"] = (env["gain"], "smem")
        refs["other"] = (env["other"], "vmem")
    outs = {}
    if backward and not last:
        outs["sum"] = ((half, nx, nz), F32)
    elif backward and final:
        outs["done"] = ((own, nx, nz), F32)
    elif backward:
        outs["est_new"] = ((half, nx, nz), F32)
        outs["image_new"] = ((half, nx, nz), BF)
    if store:
        outs["ratio_new"] = ((count, len(new), nx, nz), BF)
    scratch = []
    if backward and last:
        scratch.append(pltpu.VMEM((half, nx, nz), F32))
    if not store and backward:
        scratch.append(pltpu.VMEM((1, len(new), nx, nz), BF))

    def body(ref, scratch):
        is_odd = ref["odd"][0]
        total = None
        if backward:
            total = scratch[0] if last else ref["sum"]
            total[...] = ref["carry"][...] if carry is not None else jnp.zeros_like(total)
        fresh = ref["ratio_new"] if store else (scratch[-1] if backward else None)

        def side(q):
            return is_odd * q + (1 - is_odd) * (own - 1 - q)

        for i, (start, size, data) in enumerate(chunks):

            def step(view, _, i=i, start=start):
                weights = []
                for t in range(taps):
                    value = ref["norm"][view, is_odd * t + (1 - is_odd) * (taps - 1 - t)]
                    weights.append(jnp.full((nx, nz), value, F32).astype(BF))
                slot = view if store else 0

                def combine(rows):
                    acc = None
                    for weight, row in zip(weights, rows):
                        term = weight * row
                        acc = term if acc is None else acc + term
                    return acc

                def image(p):
                    key, q = locate_image(p, own, half)
                    held = ref[f"image_{key}{q // half}"]
                    return held[q % half] if held.shape[0] == half else held[q]

                def recorded(p):
                    if p < 0:
                        q = -1 - p
                        return ref["data_par"][view, is_odd * (half - 1 - q) + (1 - is_odd) * q]
                    if p >= own:
                        q = 2 * own - 1 - p
                        return ref[f"data_out{i}"][view - start, is_odd * (own - 1 - q) + (1 - is_odd) * (q - half)]
                    return ref["views"][view, side(p)]

                def ratio(at):
                    if at in new:
                        return fresh[slot, new.index(at)]
                    value, index = env["ratio"][at]
                    key = "ratio%d" % [id(v) for v in env["held"]].index(id(value))
                    return ref[key][view, index]

                xf, zf = ref["xf"][view], ref["zf"][view]
                for p in forward:
                    first = combine([image(p + t - ry) for t in range(taps)])
                    second = dot(xf, first).astype(BF)
                    blurred = dot(second, zf)
                    fresh[slot, new.index(p + ry)] = (recorded(p).astype(F32) / blurred).astype(BF)
                if backward:
                    xb, zb = ref["xb"][view], ref["zb"][view]
                    for j, y in enumerate(backward):
                        first = combine([ratio(y + taps - 1 - t) for t in range(taps)])
                        second = dot(xb, first).astype(BF)
                        total[j] += jnp.log(dot(second, zb))
                return 0

            lax.fori_loop(start, start + size, step, 0)
        if not (backward and last):
            return
        for j in range(half):
            value = total[j] / count
            if final:
                at = side(low_out + j)
                ref["done"][at] = ref["est"][j] * jnp.exp(value + ref["gain"][0])
                ref["done"][side((low_out + half) % own + j)] = ref["other"][j] * jnp.exp(jnp.zeros((nx, nz), F32) + ref["gain"][0])
            else:
                held = ref["est"][j] if env["oriented"] else ref["est"][side(low_out + j)]
                value = held * jnp.exp(value)
                ref["est_new"][j] = value
                ref["image_new"][j] = value.astype(BF)

    amount = sum(size for _, size, _ in chunks)
    work = 4 * nx * nz * nx * amount * (len(forward) + len(backward))
    return call(body, refs, outs, scratch, name, work)


def banded(kernel, length, flip):
    radius = kernel.shape[1] // 2
    rows = lax.broadcasted_iota(jnp.int32, (length, length), 0)
    columns = lax.broadcasted_iota(jnp.int32, (length, length), 1)
    grid = (columns - rows if flip else rows - columns) + radius
    matrix = jnp.zeros((kernel.shape[0], length, length), F32)
    for offset in range(2 * radius + 1):
        matrix = jnp.where((grid == offset)[None], kernel[:, offset][:, None, None], matrix)
    return matrix.astype(BF)


def rescaled(norm):
    factors = jnp.exp2(jnp.arange(128, dtype=F32) / 128)
    tried = norm[:, :, None] * factors
    off = lax.reduce_precision(tried, 8, 7) - tried
    cost = jnp.sum(off * off, axis=1) / (factors * factors)
    best = jnp.argmin(cost, axis=1)
    return norm * jnp.exp2(best.astype(F32) / 128)[:, None]


def after(value, other):
    return lax.optimization_barrier((value, other))[0]


def local(estimate, views_data, kernel_x, kernel_y, kernel_z):
    count = views_data.shape[0]
    own, nx, nz = estimate.shape
    half = own // 2
    ry = kernel_y.shape[1] // 2
    strip = lax.axis_size("strip")
    odd = (lax.axis_index("strip") % 2).astype(jnp.int32).reshape(1)
    pair = [(i, i ^ 1) for i in range(strip) if (i ^ 1) < strip]
    outer = []
    for i in range(1, strip - 1, 2):
        outer += [(i, i + 1), (i + 1, i)]

    def to_pair(x):
        return lax.ppermute(x, "strip", pair)

    def to_outer(x):
        return lax.ppermute(x, "strip", outer)

    sizes = list(CHUNKS) if sum(CHUNKS) == count else [1] * count
    image = orient(odd, estimate)
    image_out = to_outer(image)
    image_par = to_pair(image)
    send_a, send_b = parcel(odd, views_data, sizes)
    data_out = [to_outer(b) for b in send_b]
    data_par = to_pair(send_a)

    totals = after(sums(views_data)[:, 0], data_par)
    steps = []
    if strip & (strip - 1) == 0:
        steps = [1 << k for k in range(strip.bit_length() - 1)]
        steps = [s for s in steps if s != 2] + [s for s in steps if s == 2]

    def fold(value, step):
        return value + lax.ppermute(value, "strip", [(i, i ^ step) for i in range(strip)])

    for step in steps[:-1]:
        totals = fold(totals, step)

    norm = rescaled(kernel_y / jnp.sum(kernel_y, axis=1, keepdims=True))
    px = kernel_x / jnp.sum(kernel_x, axis=1, keepdims=True)
    pz = kernel_z / jnp.sum(kernel_z, axis=1, keepdims=True)
    env = {
        "odd": odd,
        "norm": norm,
        "mats": {
            "xf": banded(px, nx, True),
            "xb": banded(px, nx, False),
            "zf": banded(pz, nz, False),
            "zb": banded(pz, nz, True),
        },
        "views": views_data,
        "data_par": data_par,
        "image": {"own": [image, image], "par": [image_par, image_par], "out": [image_out, image_out]},
        "est": estimate,
        "oriented": False,
    }
    got = stage("inner", env, [(0, count, None)], range(-2, 4), (0, 1), store=True)
    est_a, image_a, held = got["est_new"], got["image_new"], got["ratio_new"]
    env["held"] = [held]
    env["ratio"] = {at: (held, at) for at in range(6)}
    carry, start = None, 0
    parts = []
    for i, size in enumerate(sizes):
        last = start + size == count
        parts.append((start, size, data_out[i]))
        got = stage("outer", env, parts[-1:], (4, 5), (2, 3), last=last, carry=carry)
        carry = None if last else got["sum"]
        start += size
    est_b, image_b = got["est_new"], got["image_new"]

    out_b = to_outer(image_b)
    par_a, par_b = to_pair(image_a), to_pair(image_b)
    out_a = to_outer(after(image_a, image_b))
    env.update(
        image={"own": [image_a, image_b], "par": [par_a, par_b], "out": [out_a, out_b]},
        est=est_a,
        oriented=True,
    )
    near = stage("near", env, [(0, count, None)], range(-2, 2), (), store=True)["ratio_new"]
    if steps:
        totals = fold(after(totals, near), steps[-1])
    else:
        totals = lax.psum(totals, "strip")
    weights = jnp.sum(totals) / (count * totals)
    gain = (jnp.sum(jnp.log(weights)) / count).reshape(1)
    env["held"] = [near]
    env["ratio"] = {at: (near, at) for at in range(4)}
    got = stage("middle", env, [(0, count, None)], (2, 3), (0, 1), store=True)
    middle = got["ratio_new"]
    env["held"] = [near, middle]
    env["ratio"].update({at: (middle, at - 4) for at in (4, 5)})
    env.update(est=est_b, other=got["est_new"], gain=gain)
    return stage("far", env, parts, (4, 5), (2, 3), final=True)["done"]


def solution(mesh):
    placed = (
        P(("blocks", "strip"), None, None),
        P(None, ("blocks", "strip"), None, None),
        P(),
        P(),
        P(),
    )
    return jax.shard_map(
        local,
        mesh=mesh,
        in_specs=placed,
        out_specs=P(("blocks", "strip"), None, None),
        check_vma=False,
    )
```

```python
import jax
import jax.numpy as jnp
from jax import lax
from jax.experimental import pallas as pl
from jax.experimental.pallas import tpu as pltpu
from jax.sharding import PartitionSpec as P


BF = jnp.bfloat16
F32 = jnp.float32
CHUNKS = (6, 2)
GROUP = 2
GRANT = 6 * 1024 * 1024
FULL = 60 * 1024 * 1024


def dot(left, right):
    return jnp.dot(left, right, preferred_element_type=F32)


def call(body, refs, outs, scratch, work=0, grant=GRANT):
    spaces = {"vmem": pltpu.VMEM, "smem": pltpu.SMEM, "hbm": pltpu.HBM, "any": pl.ANY}
    specs = [pl.BlockSpec(memory_space=spaces[where]) for _, where in refs.values()]
    moved = sum(value.size * value.dtype.itemsize for value, _ in refs.values())

    def kernel(*given):
        names = list(refs) + list(outs)
        body(dict(zip(names, given)), given[len(names) :])

    got = pl.pallas_call(
        kernel,
        in_specs=specs,
        out_specs=[pl.BlockSpec(memory_space=spaces[(*out, "vmem")[2]]) for out in outs.values()],
        out_shape=[jax.ShapeDtypeStruct(*out[:2]) for out in outs.values()],
        scratch_shapes=scratch,
        compiler_params=pltpu.CompilerParams(vmem_limit_bytes=grant),
        cost_estimate=pl.CostEstimate(flops=work, bytes_accessed=moved, transcendentals=0),
    )(*[value for value, _ in refs.values()])
    return dict(zip(outs, got))


def orient(odd, estimate):
    own, nx, nz = estimate.shape

    def body(ref, scratch):
        is_odd = ref["odd"][0]
        for q in range(own):
            ref["image"][q] = ref["est"][is_odd * q + (1 - is_odd) * (own - 1 - q)].astype(BF)

    refs = {"odd": (odd, "smem"), "est": (estimate, "vmem")}
    return call(body, refs, {"image": ((own, nx, nz), BF)}, [])["image"]


def parcel(odd, views, sizes):
    count, own, nx, nz = views.shape
    half = own // 2
    outs = {"a": ((count, half, nx, nz), BF)}
    outs.update({f"b{i}": ((size, half, nx, nz), BF) for i, size in enumerate(sizes)})

    def body(ref, scratch):
        is_odd = ref["odd"][0]
        sems = scratch[0]
        near, far = (1 - is_odd) * half, is_odd * half
        copies = []
        at = 0
        for i, size in enumerate(sizes):
            source = ref["views"].at[pl.ds(at, size), pl.ds(far, half)]
            copies.append(pltpu.make_async_copy(source, ref[f"b{i}"], sems.at[i]))
            at += size
        source = ref["views"].at[:, pl.ds(near, half)]
        copies.append(pltpu.make_async_copy(source, ref["a"], sems.at[len(sizes)]))
        for copy in copies:
            copy.start()
        for copy in copies:
            copy.wait()

    refs = {"odd": (odd, "smem"), "views": (views, "hbm")}
    got = call(body, refs, outs, [pltpu.SemaphoreType.DMA((len(sizes) + 1,))], grant=FULL)
    return got["a"], [got[f"b{i}"] for i in range(len(sizes))]


def sums(views):
    count, own, nx, nz = views.shape

    def body(ref, scratch):
        def step(view, _):
            total = jnp.zeros((8, nz), F32)
            for row in range(own):
                part = ref["views"][view, row].astype(F32)
                total = total + jnp.sum(part.reshape(nx // 8, 8, nz), axis=0)
            total = jnp.sum(jnp.sum(total, axis=0, keepdims=True), axis=1, keepdims=True)
            ref["total"][pl.ds(view, 1), :] = jnp.broadcast_to(total, (1, 128))
            return 0

        lax.fori_loop(0, count, step, 0)

    return call(body, {"views": (views, "vmem")}, {"total": ((count, 128), F32)}, [], grant=FULL)["total"]


def locate_image(p, own):
    if p < 0:
        key, q = "par", -1 - p
    elif p >= own:
        key, q = "out", 2 * own - 1 - p
    else:
        key, q = "own", p
    return key, q


def stage(env, chunks, forward, backward, last=True, carry=None, store=False, final=False):
    views, norm, mats = env["views"], env["norm"], env["mats"]
    count, own, nx, nz = views.shape
    taps = norm.shape[1]
    ry = taps // 2
    half = own // 2
    refs = {"odd": (env["odd"], "smem"), "norm": (norm, "smem"), "mats": (mats, "vmem")}
    reach = {locate_image(p + t - ry, own) for p in forward for t in range(taps)}
    for key, q in sorted(reach):
        value = env["image"][key][q // half]
        refs[f"image_{key}{q // half}"] = (value, "vmem")
    if any(p < 0 for p in forward):
        refs["data_par"] = (env["data_par"], "vmem")
    if any(0 <= p < own for p in forward):
        refs["views"] = (views, "vmem")
    for i, (_, _, data) in enumerate(chunks):
        if data is not None:
            refs[f"data_out{i}"] = (data, "vmem")
    new = [p + ry for p in forward]
    old = sorted({y + t for y in backward for t in range(taps)} - set(new))
    placed = {}
    for k, (value, base, rows) in enumerate(env["ratio"] if old else ()):
        for at in old:
            if base <= at < base + rows:
                refs[f"ratio{k}"] = (value, "vmem")
                placed[at] = (f"ratio{k}", at - base)
    low_out = backward[0] if backward else 0
    if backward and last:
        refs["est"] = (env["est"], "vmem")
    if carry is not None:
        refs["carry"] = (carry, "vmem")
    if final:
        refs["total_own"] = (env["totals"][0], "vmem")
        refs["total_other"] = (env["totals"][1], "vmem")
        refs["other"] = (env["other"], "vmem")
    outs = {}
    if backward and not last:
        outs["sum"] = ((half, nx, nz), F32)
    elif backward and final:
        outs["done"] = ((own, nx, nz), F32)
    elif backward:
        outs["est_new"] = ((half, nx, nz), F32)
        if not env["oriented"]:
            outs["image_new"] = ((half, nx, nz), BF)
    if store:
        outs["ratio_new"] = ((count, len(new), nx, nz), BF)
    scratch = []
    if backward and last:
        scratch.append(pltpu.VMEM((half, nx, nz), F32))
    if not store:
        scratch.append(pltpu.VMEM((GROUP, len(new), nx, nz), BF))

    def body(ref, scratch):
        is_odd = ref["odd"][0]
        fresh = ref["ratio_new"] if store else scratch[-1]
        total = None
        if backward:
            total = scratch[0] if last else ref["sum"]
            total[...] = ref["carry"][...] if carry is not None else jnp.zeros_like(total)

        def side(q):
            return is_odd * q + (1 - is_odd) * (own - 1 - q)

        def image(p):
            key, q = locate_image(p, own)
            held = ref[f"image_{key}{q // half}"]
            return held[q % half] if held.shape[0] == half else held[q]

        def blur(firsts, along_x, along_z):
            seconds = [dot(along_x, first).astype(BF) for first in firsts]
            result = dot(jnp.concatenate(seconds, axis=0), along_z)
            return [result[i * nx : (i + 1) * nx] for i in range(len(firsts))]

        for i, (start, size, _) in enumerate(chunks):

            def group(members, i=i, start=start):
                def recorded(view, p):
                    if p < 0:
                        q = -1 - p
                        return ref["data_par"][view, is_odd * (half - 1 - q) + (1 - is_odd) * q]
                    if p >= own:
                        q = 2 * own - 1 - p
                        return ref[f"data_out{i}"][view - start, is_odd * (own - 1 - q) + (1 - is_odd) * (q - half)]
                    return ref["views"][view, side(p)]

                def ratio(view, slot, row):
                    if row in new:
                        return fresh[slot, new.index(row)]
                    key, index = placed[row]
                    return ref[key][view, index]

                weights = []
                for view in members:
                    mine = []
                    for t in range(taps):
                        value = ref["norm"][view, is_odd * t + (1 - is_odd) * (taps - 1 - t)]
                        mine.append(jnp.full((nx, nz), value, F32).astype(BF))
                    weights.append(mine)

                def combine(mine, rows):
                    acc = None
                    for weight, row in zip(mine, rows):
                        term = weight * row
                        acc = term if acc is None else acc + term
                    return acc

                slots = [view if store else k for k, view in enumerate(members)]
                for mine, slot, view in zip(weights, slots, members):
                    firsts = [combine(mine, [image(p + t - ry) for t in range(taps)]) for p in forward]
                    for p, blurred in zip(forward, blur(firsts, ref["mats"][view, 0], ref["mats"][view, 1])):
                        fresh[slot, new.index(p + ry)] = (recorded(view, p).astype(F32) / blurred).astype(BF)
                if not backward:
                    return
                product = [None] * len(backward)
                for mine, slot, view in zip(weights, slots, members):
                    firsts = [combine(mine, [ratio(view, slot, y + taps - 1 - t) for t in range(taps)]) for y in backward]
                    for j, value in enumerate(blur(firsts, ref["mats"][view, 2], ref["mats"][view, 3])):
                        product[j] = value if product[j] is None else product[j] * value
                for j, value in enumerate(product):
                    total[j] += jnp.log(value)

            def step(k, _, start=start):
                group([start + GROUP * k + m for m in range(GROUP)])
                return 0

            lax.fori_loop(0, size // GROUP, step, 0)
            for view in range(start + size // GROUP * GROUP, start + size):
                group([view])
        if not (backward and last):
            return
        if final:
            sums_all = ref["total_own"][...] + ref["total_other"][...]
            shares = jnp.sum(sums_all, axis=0, keepdims=True) / (count * sums_all)
            gain = jnp.sum(jnp.log(shares), axis=0, keepdims=True) / count
            gain = jnp.concatenate([gain] * (nz // 128), axis=1)
            factor = jnp.exp(gain)
        for j in range(half):
            value = total[j] / count
            if final:
                ref["done"][side(low_out + j)] = ref["est"][j] * jnp.exp(value + gain)
                ref["done"][side((low_out + half) % own + j)] = ref["other"][j] * factor
            else:
                held = ref["est"][j] if env["oriented"] else ref["est"][side(low_out + j)]
                value = held * jnp.exp(value)
                ref["est_new"][j] = value
                if not env["oriented"]:
                    ref["image_new"][j] = value.astype(BF)

    amount = sum(size for _, size, _ in chunks)
    work = 4 * nx * nz * nx * amount * (len(forward) + len(backward))
    return call(body, refs, outs, scratch, work)


def matrices(px, pz, length):
    count, taps = px.shape
    radius = taps // 2

    def body(ref, scratch):
        rows = lax.broadcasted_iota(jnp.int32, (length, length), 0)
        columns = lax.broadcasted_iota(jnp.int32, (length, length), 1)
        for flip in (False, True):
            grid = (columns - rows if flip else rows - columns) + radius
            for key, slot in (("x", 0 if flip else 2), ("z", 3 if flip else 1)):

                def step(view, _, grid=grid, key=key, slot=slot):
                    matrix = jnp.zeros((length, length), F32)
                    for offset in range(taps):
                        matrix = jnp.where(grid == offset, ref[key][view, offset], matrix)
                    ref["mats"][view, slot] = matrix.astype(BF)
                    return 0

                lax.fori_loop(0, count, step, 0)

    refs = {"x": (px, "smem"), "z": (pz, "smem")}
    return call(body, refs, {"mats": ((count, 4, length, length), BF)}, [])["mats"]


def rescaled(norm):
    factors = jnp.exp2(jnp.arange(128, dtype=F32) / 128)
    tried = norm[:, :, None] * factors
    off = lax.reduce_precision(tried, 8, 7) - tried
    cost = jnp.sum(off * off, axis=1) / (factors * factors)
    best = jnp.argmin(cost, axis=1)
    return norm * jnp.exp2(best.astype(F32) / 128)[:, None]


def after(value, other):
    return lax.optimization_barrier((value, other))[0]


def local(estimate, views_data, kernel_x, kernel_y, kernel_z):
    count = views_data.shape[0]
    _, nx, _ = estimate.shape
    strip = lax.axis_size("strip")
    odd = (lax.axis_index("strip") % 2).astype(jnp.int32).reshape(1)
    pair = [(i, i ^ 1) for i in range(strip) if (i ^ 1) < strip]
    outer = []
    for i in range(1, strip - 1, 2):
        outer += [(i, i + 1), (i + 1, i)]

    def to_pair(x):
        return lax.ppermute(x, "strip", pair)

    def to_outer(x):
        return lax.ppermute(x, "strip", outer)

    sizes = list(CHUNKS) if sum(CHUNKS) == count else [1] * count
    image = orient(odd, estimate)
    image_out = to_outer(image)
    image_par = to_pair(image)
    send_a, send_b = parcel(odd, views_data, sizes)
    data_out = [to_outer(b) for b in send_b]
    data_par = to_pair(send_a)

    totals = sums(views_data)
    steps = []
    if strip > 1 and strip & (strip - 1) == 0:
        steps = [1 << k for k in range(strip.bit_length() - 1)]
        steps = [1] + [s for s in steps if s > 2] + [s for s in steps if s == 2]

    def fold(value, step):
        return lax.ppermute(value, "strip", [(i, i ^ step) for i in range(strip)])

    norm = after(rescaled(kernel_y / jnp.sum(kernel_y, axis=1, keepdims=True)), totals)
    px = kernel_x / jnp.sum(kernel_x, axis=1, keepdims=True)
    pz = kernel_z / jnp.sum(kernel_z, axis=1, keepdims=True)
    env = {
        "odd": odd,
        "norm": norm,
        "mats": matrices(px, pz, nx),
        "views": views_data,
        "data_par": data_par,
        "image": {"own": [image, image], "par": [image_par, image_par], "out": [image_out, image_out]},
        "est": estimate,
        "oriented": False,
    }
    got = stage(env, [(0, count, None)], range(-2, 4), (0, 1), store=True)
    est_a, image_a, held = got["est_new"], got["image_new"], got["ratio_new"]
    env["ratio"] = [(held, 0, 6)]
    carry, start = None, 0
    parts, par_a = [], None
    queue = list(steps)
    for i, size in enumerate(sizes):
        last = start + size == count
        parts.append((start, size, data_out[i]))
        if last and carry is not None:
            par_a = to_pair(after(image_a, carry))
            if queue:
                totals = totals + fold(after(totals, carry), queue.pop(0))
            carry, par_a, totals = lax.optimization_barrier((carry, par_a, totals))
        got = stage(env, parts[-1:], (4, 5), (2, 3), last=last, carry=carry)
        carry = None if last else got["sum"]
        start += size
    est_b, image_b = got["est_new"], got["image_new"]
    if par_a is None:
        par_a = to_pair(image_a)

    out_b = to_outer(image_b)
    par_b = to_pair(image_b)
    while len(queue) > 3:
        totals = totals + fold(after(totals, image_b), queue.pop(0))
    if len(queue) > 2:
        seen = fold(after(totals, image_b), queue.pop(0))
    else:
        seen = None
    env.update(
        image={"own": [image_a, image_b], "par": [par_a, par_b], "out": [None, out_b]},
        est=est_a,
        oriented=True,
    )
    near = stage(env, [(0, count, None)], range(-2, 2), (), store=True)["ratio_new"]
    out_a = to_outer(after(image_a, near))
    if seen is not None:
        totals = totals + after(seen, near)
    if len(queue) > 1:
        seen = fold(after(totals, near), queue.pop(0))
    else:
        seen = None
    env["image"]["out"][0] = out_a
    env["ratio"] = [(near, 0, 4)]
    got = stage(env, [(0, count, None)], (2, 3), (0, 1), store=True)
    middle = got["ratio_new"]
    if seen is not None:
        totals = totals + after(seen, middle)
    if queue:
        other = fold(after(totals, middle), queue.pop(0))
    else:
        totals = totals if steps else lax.psum(totals, "strip")
        other = jnp.zeros_like(totals)
    env["totals"] = (totals, other)
    env["ratio"] = [(near, 0, 4), (middle, 4, 2)]
    env.update(est=est_b, other=got["est_new"])
    return stage(env, parts, (4, 5), (2, 3), final=True)["done"]


def solution(mesh):
    placed = (
        P(("blocks", "strip"), None, None),
        P(None, ("blocks", "strip"), None, None),
        P(),
        P(),
        P(),
    )

    return jax.shard_map(
        local,
        mesh=mesh,
        in_specs=placed,
        out_specs=P(("blocks", "strip"), None, None),
        check_vma=False,
    )
```

```python
import jax
import jax.numpy as jnp
from jax import lax
from jax.experimental import pallas as pl
from jax.experimental.pallas import tpu as pltpu
from jax.sharding import PartitionSpec as P


BF = jnp.bfloat16
F32 = jnp.float32
CHUNKS = (7, 1)
GROUP = 2
GRANT = 6 * 1024 * 1024
FULL = 60 * 1024 * 1024


def dot(left, right):
    return jnp.dot(left, right, preferred_element_type=F32)


def call(body, refs, outs, scratch, work=0, grant=GRANT):
    spaces = {"vmem": pltpu.VMEM, "smem": pltpu.SMEM, "hbm": pltpu.HBM, "any": pl.ANY}
    specs = [pl.BlockSpec(memory_space=spaces[where]) for _, where in refs.values()]
    moved = sum(value.size * value.dtype.itemsize for value, _ in refs.values())

    def kernel(*given):
        names = list(refs) + list(outs)
        body(dict(zip(names, given)), given[len(names) :])

    got = pl.pallas_call(
        kernel,
        in_specs=specs,
        out_specs=[pl.BlockSpec(memory_space=spaces[(*out, "vmem")[2]]) for out in outs.values()],
        out_shape=[jax.ShapeDtypeStruct(*out[:2]) for out in outs.values()],
        scratch_shapes=scratch,
        compiler_params=pltpu.CompilerParams(vmem_limit_bytes=grant),
        cost_estimate=pl.CostEstimate(flops=work, bytes_accessed=moved, transcendentals=0),
    )(*[value for value, _ in refs.values()])
    return dict(zip(outs, got))


def orient(odd, estimate):
    own, nx, nz = estimate.shape

    def body(ref, scratch):
        is_odd = ref["odd"][0]
        for q in range(own):
            ref["image"][q] = ref["est"][is_odd * q + (1 - is_odd) * (own - 1 - q)].astype(BF)

    refs = {"odd": (odd, "smem"), "est": (estimate, "vmem")}
    return call(body, refs, {"image": ((own, nx, nz), BF)}, [])["image"]


def parcel(odd, views, sizes):
    count, own, nx, nz = views.shape
    half = own // 2
    outs = {"a": ((count, half, nx, nz), BF)}
    outs.update({f"b{i}": ((size, half, nx, nz), BF) for i, size in enumerate(sizes)})

    def body(ref, scratch):
        is_odd = ref["odd"][0]
        sems = scratch[0]
        near, far = (1 - is_odd) * half, is_odd * half
        copies = []
        at = 0
        for i, size in enumerate(sizes):
            source = ref["views"].at[pl.ds(at, size), pl.ds(far, half)]
            copies.append(pltpu.make_async_copy(source, ref[f"b{i}"], sems.at[i]))
            at += size
        source = ref["views"].at[:, pl.ds(near, half)]
        copies.append(pltpu.make_async_copy(source, ref["a"], sems.at[len(sizes)]))
        for copy in copies:
            copy.start()
        for copy in copies:
            copy.wait()

    refs = {"odd": (odd, "smem"), "views": (views, "hbm")}
    got = call(body, refs, outs, [pltpu.SemaphoreType.DMA((len(sizes) + 1,))], grant=FULL)
    return got["a"], [got[f"b{i}"] for i in range(len(sizes))]


def sums(views):
    count, own, nx, nz = views.shape

    def body(ref, scratch):
        def step(view, _):
            total = jnp.zeros((8, nz), F32)
            for row in range(own):
                part = ref["views"][view, row].astype(F32)
                total = total + jnp.sum(part.reshape(nx // 8, 8, nz), axis=0)
            total = jnp.sum(jnp.sum(total, axis=0, keepdims=True), axis=1, keepdims=True)
            ref["total"][pl.ds(view, 1), :] = jnp.broadcast_to(total, (1, 128))
            return 0

        lax.fori_loop(0, count, step, 0)

    return call(body, {"views": (views, "vmem")}, {"total": ((count, 128), F32)}, [], grant=FULL)["total"]


def locate_image(p, own):
    if p < 0:
        key, q = "par", -1 - p
    elif p >= own:
        key, q = "out", 2 * own - 1 - p
    else:
        key, q = "own", p
    return key, q


def stage(env, chunks, forward, backward, last=True, carry=None, store=False, final=False):
    views, norm, mats = env["views"], env["norm"], env["mats"]
    count, own, nx, nz = views.shape
    taps = norm.shape[1]
    ry = taps // 2
    half = own // 2
    refs = {"odd": (env["odd"], "smem"), "norm": (norm, "smem"), "mats": (mats, "vmem")}
    reach = {locate_image(p + t - ry, own) for p in forward for t in range(taps)}
    for key, q in sorted(reach):
        value = env["image"][key][q // half]
        refs[f"image_{key}{q // half}"] = (value, "vmem")
    if any(p < 0 for p in forward):
        refs["data_par"] = (env["data_par"], "vmem")
    if any(0 <= p < own for p in forward):
        refs["views"] = (views, "vmem")
    for i, (_, _, data) in enumerate(chunks):
        if data is not None:
            refs[f"data_out{i}"] = (data, "vmem")
    new = [p + ry for p in forward]
    old = sorted({y + t for y in backward for t in range(taps)} - set(new))
    placed = {}
    for k, (value, base, rows) in enumerate(env["ratio"] if old else ()):
        for at in old:
            if base <= at < base + rows:
                refs[f"ratio{k}"] = (value, "vmem")
                placed[at] = (f"ratio{k}", at - base)
    low_out = backward[0] if backward else 0
    if backward and last:
        refs["est"] = (env["est"], "vmem")
    if carry is not None:
        refs["carry"] = (carry, "vmem")
    if final:
        refs["total_own"] = (env["totals"][0], "vmem")
        refs["total_other"] = (env["totals"][1], "vmem")
        refs["other"] = (env["other"], "vmem")
    outs = {}
    if backward and not last:
        outs["sum"] = ((half, nx, nz), F32)
    elif backward and final:
        outs["done"] = ((own, nx, nz), F32)
    elif backward:
        outs["est_new"] = ((half, nx, nz), F32)
        if not env["oriented"]:
            outs["image_new"] = ((half, nx, nz), BF)
    if store:
        outs["ratio_new"] = ((count, len(new), nx, nz), BF)
    scratch = []
    if backward and last:
        scratch.append(pltpu.VMEM((half, nx, nz), F32))
    if not store:
        scratch.append(pltpu.VMEM((GROUP, len(new), nx, nz), BF))

    def body(ref, scratch):
        is_odd = ref["odd"][0]
        fresh = ref["ratio_new"] if store else scratch[-1]
        total = None
        if backward:
            total = scratch[0] if last else ref["sum"]
            total[...] = ref["carry"][...] if carry is not None else jnp.zeros_like(total)

        def side(q):
            return is_odd * q + (1 - is_odd) * (own - 1 - q)

        def image(p):
            key, q = locate_image(p, own)
            held = ref[f"image_{key}{q // half}"]
            return held[q % half] if held.shape[0] == half else held[q]

        def blur(firsts, along_x, along_z):
            seconds = [dot(along_x, first).astype(BF) for first in firsts]
            result = dot(jnp.concatenate(seconds, axis=0), along_z)
            return [result[i * nx : (i + 1) * nx] for i in range(len(firsts))]

        for i, (start, size, _) in enumerate(chunks):

            def group(members, i=i, start=start):
                def recorded(view, p):
                    if p < 0:
                        q = -1 - p
                        return ref["data_par"][view, is_odd * (half - 1 - q) + (1 - is_odd) * q]
                    if p >= own:
                        q = 2 * own - 1 - p
                        return ref[f"data_out{i}"][view - start, is_odd * (own - 1 - q) + (1 - is_odd) * (q - half)]
                    return ref["views"][view, side(p)]

                def ratio(view, slot, row):
                    if row in new:
                        return fresh[slot, new.index(row)]
                    key, index = placed[row]
                    return ref[key][view, index]

                weights = []
                for view in members:
                    mine = []
                    for t in range(taps):
                        value = ref["norm"][view, is_odd * t + (1 - is_odd) * (taps - 1 - t)]
                        mine.append(jnp.full((nx, nz), value, F32).astype(BF))
                    weights.append(mine)

                def combine(mine, rows):
                    acc = None
                    for weight, row in zip(mine, rows):
                        term = weight * row
                        acc = term if acc is None else acc + term
                    return acc

                slots = [view if store else k for k, view in enumerate(members)]
                for mine, slot, view in zip(weights, slots, members):
                    firsts = [combine(mine, [image(p + t - ry) for t in range(taps)]) for p in forward]
                    for p, blurred in zip(forward, blur(firsts, ref["mats"][view, 0], ref["mats"][view, 1])):
                        fresh[slot, new.index(p + ry)] = (recorded(view, p).astype(F32) / blurred).astype(BF)
                if not backward:
                    return
                product = [None] * len(backward)
                for mine, slot, view in zip(weights, slots, members):
                    firsts = [combine(mine, [ratio(view, slot, y + taps - 1 - t) for t in range(taps)]) for y in backward]
                    for j, value in enumerate(blur(firsts, ref["mats"][view, 2], ref["mats"][view, 3])):
                        product[j] = value if product[j] is None else product[j] * value
                for j, value in enumerate(product):
                    total[j] += jnp.log(value)

            def step(k, _, start=start):
                group([start + GROUP * k + m for m in range(GROUP)])
                return 0

            lax.fori_loop(0, size // GROUP, step, 0)
            for view in range(start + size // GROUP * GROUP, start + size):
                group([view])
        if not (backward and last):
            return
        if final:
            sums_all = ref["total_own"][...] + ref["total_other"][...]
            shares = jnp.sum(sums_all, axis=0, keepdims=True) / (count * sums_all)
            gain = jnp.sum(jnp.log(shares), axis=0, keepdims=True) / count
            gain = jnp.concatenate([gain] * (nz // 128), axis=1)
            factor = jnp.exp(gain)
        for j in range(half):
            value = total[j] / count
            if final:
                ref["done"][side(low_out + j)] = ref["est"][j] * jnp.exp(value + gain)
                ref["done"][side((low_out + half) % own + j)] = ref["other"][j] * factor
            else:
                held = ref["est"][j] if env["oriented"] else ref["est"][side(low_out + j)]
                value = held * jnp.exp(value)
                ref["est_new"][j] = value
                if not env["oriented"]:
                    ref["image_new"][j] = value.astype(BF)

    amount = sum(size for _, size, _ in chunks)
    work = 4 * nx * nz * nx * amount * (len(forward) + len(backward))
    return call(body, refs, outs, scratch, work)


def matrices(px, pz, length):
    count, taps = px.shape
    radius = taps // 2

    def body(ref, scratch):
        rows = lax.broadcasted_iota(jnp.int32, (length, length), 0)
        columns = lax.broadcasted_iota(jnp.int32, (length, length), 1)
        for flip in (False, True):
            grid = (columns - rows if flip else rows - columns) + radius
            for key, slot in (("x", 0 if flip else 2), ("z", 3 if flip else 1)):

                def step(view, _, grid=grid, key=key, slot=slot):
                    matrix = jnp.zeros((length, length), F32)
                    for offset in range(taps):
                        matrix = jnp.where(grid == offset, ref[key][view, offset], matrix)
                    ref["mats"][view, slot] = matrix.astype(BF)
                    return 0

                lax.fori_loop(0, count, step, 0)

    refs = {"x": (px, "smem"), "z": (pz, "smem")}
    return call(body, refs, {"mats": ((count, 4, length, length), BF)}, [])["mats"]


def rescaled(norm):
    factors = jnp.exp2(jnp.arange(128, dtype=F32) / 128)
    tried = norm[:, :, None] * factors
    off = lax.reduce_precision(tried, 8, 7) - tried
    cost = jnp.sum(off * off, axis=1) / (factors * factors)
    best = jnp.argmin(cost, axis=1)
    return norm * jnp.exp2(best.astype(F32) / 128)[:, None]


def after(value, other):
    return lax.optimization_barrier((value, other))[0]


def local(estimate, views_data, kernel_x, kernel_y, kernel_z):
    count = views_data.shape[0]
    _, nx, _ = estimate.shape
    strip = lax.axis_size("strip")
    odd = (lax.axis_index("strip") % 2).astype(jnp.int32).reshape(1)
    pair = [(i, i ^ 1) for i in range(strip) if (i ^ 1) < strip]
    outer = []
    for i in range(1, strip - 1, 2):
        outer += [(i, i + 1), (i + 1, i)]

    def to_pair(x):
        return lax.ppermute(x, "strip", pair)

    def to_outer(x):
        return lax.ppermute(x, "strip", outer)

    sizes = list(CHUNKS) if sum(CHUNKS) == count else [1] * count
    image = orient(odd, estimate)
    image_out = to_outer(image)
    image_par = to_pair(image)
    send_a, send_b = parcel(odd, views_data, sizes)
    data_out = [to_outer(b) for b in send_b]
    data_par = to_pair(send_a)

    totals = sums(views_data)
    steps = []
    if strip > 1 and strip & (strip - 1) == 0:
        steps = [1 << k for k in range(strip.bit_length() - 1)]
        steps = [1] + [s for s in steps if s > 2] + [s for s in steps if s == 2]

    def fold(value, step):
        return lax.ppermute(value, "strip", [(i, i ^ step) for i in range(strip)])

    norm = after(rescaled(kernel_y / jnp.sum(kernel_y, axis=1, keepdims=True)), totals)
    px = kernel_x / jnp.sum(kernel_x, axis=1, keepdims=True)
    pz = kernel_z / jnp.sum(kernel_z, axis=1, keepdims=True)
    env = {
        "odd": odd,
        "norm": norm,
        "mats": matrices(px, pz, nx),
        "views": views_data,
        "data_par": data_par,
        "image": {"own": [image, image], "par": [image_par, image_par], "out": [image_out, image_out]},
        "est": estimate,
        "oriented": False,
    }
    got = stage(env, [(0, count, None)], range(-2, 4), (0, 1), store=True)
    est_a, image_a, held = got["est_new"], got["image_new"], got["ratio_new"]
    par_a = to_pair(image_a)
    if steps:
        totals = after(totals, image_a)
        for step in steps[:-1]:
            totals = totals + fold(totals, step)
        held = after(held, totals)
    env["ratio"] = [(held, 0, 6)]
    carry, start, parts = None, 0, []
    for i, size in enumerate(sizes):
        last = start + size == count
        parts.append((start, size, data_out[i]))
        got = stage(env, parts[-1:], (4, 5), (2, 3), last=last, carry=carry)
        carry = None if last else got["sum"]
        start += size
    est_b, image_b = got["est_new"], got["image_new"]

    out_b = to_outer(image_b)
    par_b = to_pair(image_b)
    out_a = to_outer(after(image_a, image_b))
    env.update(
        image={"own": [image_a, image_b], "par": [par_a, par_b], "out": [out_a, out_b]},
        est=est_a,
        oriented=True,
    )
    near = stage(env, [(0, count, None)], range(-2, 2), (), store=True)["ratio_new"]
    if steps:
        totals = after(totals, near)
        other = fold(totals, steps[-1])
    else:
        totals = lax.psum(totals, "strip")
        other = jnp.zeros_like(totals)
    env["ratio"] = [(near, 0, 4)]
    got = stage(env, [(0, count, None)], (2, 3), (0, 1), store=True)
    middle = got["ratio_new"]
    env["totals"] = (totals, other)
    env["ratio"] = [(near, 0, 4), (middle, 4, 2)]
    env.update(est=est_b, other=got["est_new"])
    return stage(env, parts, (4, 5), (2, 3), final=True)["done"]


def solution(mesh):
    placed = (
        P(("blocks", "strip"), None, None),
        P(None, ("blocks", "strip"), None, None),
        P(),
        P(),
        P(),
    )

    return jax.shard_map(
        local,
        mesh=mesh,
        in_specs=placed,
        out_specs=P(("blocks", "strip"), None, None),
        check_vma=False,
    )
```

```python
import jax
import jax.numpy as jnp
from jax import lax
from jax.experimental import pallas as pl
from jax.experimental.pallas import tpu as pltpu
from jax.sharding import PartitionSpec as P


BF = jnp.bfloat16
F32 = jnp.float32
CHUNKS = (6, 2)
GROUP = 2
GRANT = 6 * 1024 * 1024
FULL = 60 * 1024 * 1024


def dot(left, right):
    return jnp.dot(left, right, preferred_element_type=F32)


def call(body, refs, outs, scratch, work=0, grant=GRANT):
    spaces = {"vmem": pltpu.VMEM, "smem": pltpu.SMEM, "hbm": pltpu.HBM, "any": pl.ANY}
    specs = [pl.BlockSpec(memory_space=spaces[where]) for _, where in refs.values()]
    moved = sum(value.size * value.dtype.itemsize for value, _ in refs.values())

    def kernel(*given):
        names = list(refs) + list(outs)
        body(dict(zip(names, given)), given[len(names) :])

    got = pl.pallas_call(
        kernel,
        in_specs=specs,
        out_specs=[pl.BlockSpec(memory_space=spaces[(*out, "vmem")[2]]) for out in outs.values()],
        out_shape=[jax.ShapeDtypeStruct(*out[:2]) for out in outs.values()],
        scratch_shapes=scratch,
        compiler_params=pltpu.CompilerParams(vmem_limit_bytes=grant),
        cost_estimate=pl.CostEstimate(flops=work, bytes_accessed=moved, transcendentals=0),
    )(*[value for value, _ in refs.values()])
    return dict(zip(outs, got))


def orient(odd, estimate):
    own, nx, nz = estimate.shape

    def body(ref, scratch):
        is_odd = ref["odd"][0]
        for q in range(own):
            ref["image"][q] = ref["est"][is_odd * q + (1 - is_odd) * (own - 1 - q)].astype(BF)

    refs = {"odd": (odd, "smem"), "est": (estimate, "vmem")}
    return call(body, refs, {"image": ((own, nx, nz), BF)}, [])["image"]


def parcel(odd, views, sizes):
    count, own, nx, nz = views.shape
    half = own // 2
    outs = {"a": ((count, half, nx, nz), BF)}
    outs.update({f"b{i}": ((size, half, nx, nz), BF) for i, size in enumerate(sizes)})

    def body(ref, scratch):
        is_odd = ref["odd"][0]
        sems = scratch[0]
        near, far = (1 - is_odd) * half, is_odd * half
        copies = []
        at = 0
        for i, size in enumerate(sizes):
            source = ref["views"].at[pl.ds(at, size), pl.ds(far, half)]
            copies.append(pltpu.make_async_copy(source, ref[f"b{i}"], sems.at[i]))
            at += size
        source = ref["views"].at[:, pl.ds(near, half)]
        copies.append(pltpu.make_async_copy(source, ref["a"], sems.at[len(sizes)]))
        for copy in copies:
            copy.start()
        for copy in copies:
            copy.wait()

    refs = {"odd": (odd, "smem"), "views": (views, "hbm")}
    got = call(body, refs, outs, [pltpu.SemaphoreType.DMA((len(sizes) + 1,))], grant=FULL)
    return got["a"], [got[f"b{i}"] for i in range(len(sizes))]


def sums(views):
    count, own, nx, nz = views.shape

    def body(ref, scratch):
        def step(view, _):
            total = jnp.zeros((8, nz), F32)
            for row in range(own):
                part = ref["views"][view, row].astype(F32)
                total = total + jnp.sum(part.reshape(nx // 8, 8, nz), axis=0)
            total = jnp.sum(jnp.sum(total, axis=0, keepdims=True), axis=1, keepdims=True)
            ref["total"][pl.ds(view, 1), :] = jnp.broadcast_to(total, (1, 128))
            return 0

        lax.fori_loop(0, count, step, 0)

    return call(body, {"views": (views, "vmem")}, {"total": ((count, 128), F32)}, [], grant=FULL)["total"]


def locate_image(p, own):
    if p < 0:
        key, q = "par", -1 - p
    elif p >= own:
        key, q = "out", 2 * own - 1 - p
    else:
        key, q = "own", p
    return key, q


def stage(env, chunks, forward, backward, last=True, carry=None, store=False, final=False):
    views, norm, mats = env["views"], env["norm"], env["mats"]
    count, own, nx, nz = views.shape
    taps = norm.shape[1]
    ry = taps // 2
    half = own // 2
    refs = {"odd": (env["odd"], "smem"), "norm": (norm, "smem"), "mats": (mats, "vmem")}
    reach = {locate_image(p + t - ry, own) for p in forward for t in range(taps)}
    for key, q in sorted(reach):
        value = env["image"][key][q // half]
        refs[f"image_{key}{q // half}"] = (value, "vmem")
    if any(p < 0 for p in forward):
        refs["data_par"] = (env["data_par"], "vmem")
    if any(0 <= p < own for p in forward):
        refs["views"] = (views, "vmem")
    for i, (_, _, data) in enumerate(chunks):
        if data is not None:
            refs[f"data_out{i}"] = (data, "vmem")
    new = [p + ry for p in forward]
    old = sorted({y + t for y in backward for t in range(taps)} - set(new))
    placed = {}
    for k, (value, base, rows) in enumerate(env["ratio"] if old else ()):
        for at in old:
            if base <= at < base + rows:
                refs[f"ratio{k}"] = (value, "vmem")
                placed[at] = (f"ratio{k}", at - base)
    low_out = backward[0] if backward else 0
    if backward and last:
        refs["est"] = (env["est"], "vmem")
    if carry is not None:
        refs["carry"] = (carry, "vmem")
    if final:
        refs["total_own"] = (env["totals"][0], "vmem")
        refs["total_other"] = (env["totals"][1], "vmem")
        refs["other"] = (env["other"], "vmem")
    outs = {}
    if backward and not last:
        outs["sum"] = ((half, nx, nz), F32)
    elif backward and final:
        outs["done"] = ((own, nx, nz), F32)
    elif backward:
        outs["est_new"] = ((half, nx, nz), F32)
        if not env["oriented"]:
            outs["image_new"] = ((half, nx, nz), BF)
    if store:
        outs["ratio_new"] = ((count, len(new), nx, nz), BF)
    scratch = []
    if backward and last:
        scratch.append(pltpu.VMEM((half, nx, nz), F32))
    if not store:
        scratch.append(pltpu.VMEM((GROUP, len(new), nx, nz), BF))

    def body(ref, scratch):
        is_odd = ref["odd"][0]
        fresh = ref["ratio_new"] if store else scratch[-1]
        total = None
        if backward:
            total = scratch[0] if last else ref["sum"]
            total[...] = ref["carry"][...] if carry is not None else jnp.zeros_like(total)

        def side(q):
            return is_odd * q + (1 - is_odd) * (own - 1 - q)

        def image(p):
            key, q = locate_image(p, own)
            held = ref[f"image_{key}{q // half}"]
            return held[q % half] if held.shape[0] == half else held[q]

        def blur(firsts, along_x, along_z):
            seconds = [dot(along_x, first).astype(BF) for first in firsts]
            result = dot(jnp.concatenate(seconds, axis=0), along_z)
            return [result[i * nx : (i + 1) * nx] for i in range(len(firsts))]

        for i, (start, size, _) in enumerate(chunks):

            def group(members, i=i, start=start):
                def recorded(view, p):
                    if p < 0:
                        q = -1 - p
                        return ref["data_par"][view, is_odd * (half - 1 - q) + (1 - is_odd) * q]
                    if p >= own:
                        q = 2 * own - 1 - p
                        return ref[f"data_out{i}"][view - start, is_odd * (own - 1 - q) + (1 - is_odd) * (q - half)]
                    return ref["views"][view, side(p)]

                def ratio(view, slot, row):
                    if row in new:
                        return fresh[slot, new.index(row)]
                    key, index = placed[row]
                    return ref[key][view, index]

                weights = []
                for view in members:
                    mine = []
                    for t in range(taps):
                        value = ref["norm"][view, is_odd * t + (1 - is_odd) * (taps - 1 - t)]
                        mine.append(jnp.full((nx, nz), value, F32).astype(BF))
                    weights.append(mine)

                def combine(mine, rows):
                    acc = None
                    for weight, row in zip(mine, rows):
                        term = weight * row
                        acc = term if acc is None else acc + term
                    return acc

                slots = [view if store else k for k, view in enumerate(members)]
                for mine, slot, view in zip(weights, slots, members):
                    firsts = [combine(mine, [image(p + t - ry) for t in range(taps)]) for p in forward]
                    for p, blurred in zip(forward, blur(firsts, ref["mats"][view, 0], ref["mats"][view, 1])):
                        fresh[slot, new.index(p + ry)] = (recorded(view, p).astype(F32) / blurred).astype(BF)
                if not backward:
                    return
                product = [None] * len(backward)
                for mine, slot, view in zip(weights, slots, members):
                    firsts = [combine(mine, [ratio(view, slot, y + taps - 1 - t) for t in range(taps)]) for y in backward]
                    for j, value in enumerate(blur(firsts, ref["mats"][view, 2], ref["mats"][view, 3])):
                        product[j] = value if product[j] is None else product[j] * value
                for j, value in enumerate(product):
                    total[j] += jnp.log(value)

            def step(k, _, start=start):
                group([start + GROUP * k + m for m in range(GROUP)])
                return 0

            lax.fori_loop(0, size // GROUP, step, 0)
            for view in range(start + size // GROUP * GROUP, start + size):
                group([view])
        if not (backward and last):
            return
        if final:
            sums_all = ref["total_own"][...] + ref["total_other"][...]
            shares = jnp.sum(sums_all, axis=0, keepdims=True) / (count * sums_all)
            gain = jnp.sum(jnp.log(shares), axis=0, keepdims=True) / count
            gain = jnp.concatenate([gain] * (nz // 128), axis=1)
            factor = jnp.exp(gain)
        for j in range(half):
            value = total[j] / count
            if final:
                ref["done"][side(low_out + j)] = ref["est"][j] * jnp.exp(value + gain)
                ref["done"][side((low_out + half) % own + j)] = ref["other"][j] * factor
            else:
                held = ref["est"][j] if env["oriented"] else ref["est"][side(low_out + j)]
                value = held * jnp.exp(value)
                ref["est_new"][j] = value
                if not env["oriented"]:
                    ref["image_new"][j] = value.astype(BF)

    amount = sum(size for _, size, _ in chunks)
    work = 4 * nx * nz * nx * amount * (len(forward) + len(backward))
    return call(body, refs, outs, scratch, work)


def matrices(px, pz, length):
    count, taps = px.shape
    radius = taps // 2

    def body(ref, scratch):
        rows = lax.broadcasted_iota(jnp.int32, (length, length), 0)
        columns = lax.broadcasted_iota(jnp.int32, (length, length), 1)
        for flip in (False, True):
            grid = (columns - rows if flip else rows - columns) + radius
            for key, slot in (("x", 0 if flip else 2), ("z", 3 if flip else 1)):

                def step(view, _, grid=grid, key=key, slot=slot):
                    matrix = jnp.zeros((length, length), F32)
                    for offset in range(taps):
                        matrix = jnp.where(grid == offset, ref[key][view, offset], matrix)
                    ref["mats"][view, slot] = matrix.astype(BF)
                    return 0

                lax.fori_loop(0, count, step, 0)

    refs = {"x": (px, "smem"), "z": (pz, "smem")}
    return call(body, refs, {"mats": ((count, 4, length, length), BF)}, [])["mats"]


def rescaled(norm):
    factors = jnp.exp2(jnp.arange(128, dtype=F32) / 128)
    tried = norm[:, :, None] * factors
    off = lax.reduce_precision(tried, 8, 7) - tried
    cost = jnp.sum(off * off, axis=1) / (factors * factors)
    best = jnp.argmin(cost, axis=1)
    return norm * jnp.exp2(best.astype(F32) / 128)[:, None]


def after(value, other):
    return lax.optimization_barrier((value, other))[0]


def local(estimate, views_data, kernel_x, kernel_y, kernel_z):
    count = views_data.shape[0]
    _, nx, _ = estimate.shape
    strip = lax.axis_size("strip")
    odd = (lax.axis_index("strip") % 2).astype(jnp.int32).reshape(1)
    pair = [(i, i ^ 1) for i in range(strip) if (i ^ 1) < strip]
    outer = []
    for i in range(1, strip - 1, 2):
        outer += [(i, i + 1), (i + 1, i)]

    def to_pair(x):
        return lax.ppermute(x, "strip", pair)

    def to_outer(x):
        return lax.ppermute(x, "strip", outer)

    sizes = list(CHUNKS) if sum(CHUNKS) == count else [1] * count
    image = orient(odd, estimate)
    image_out = to_outer(image)
    image_par = to_pair(image)
    send_a, send_b = parcel(odd, views_data, sizes)
    data_out = [to_outer(b) for b in send_b]
    data_par = to_pair(send_a)

    totals = sums(views_data)
    steps = []
    if strip > 1 and strip & (strip - 1) == 0:
        steps = [1 << k for k in range(strip.bit_length() - 1)]
        steps = [1] + [s for s in steps if s > 2] + [s for s in steps if s == 2]

    def fold(value, step):
        return lax.ppermute(value, "strip", [(i, i ^ step) for i in range(strip)])

    norm = rescaled(kernel_y / jnp.sum(kernel_y, axis=1, keepdims=True))
    px = kernel_x / jnp.sum(kernel_x, axis=1, keepdims=True)
    pz = kernel_z / jnp.sum(kernel_z, axis=1, keepdims=True)
    px, pz, norm, totals = lax.optimization_barrier((px, pz, norm, totals))
    mats = matrices(px, pz, nx)
    totals = after(totals, mats)
    for step in steps[:-1]:
        totals = totals + fold(totals, step)
    norm = after(norm, totals)
    env = {
        "odd": odd,
        "norm": norm,
        "mats": mats,
        "views": views_data,
        "data_par": data_par,
        "image": {"own": [image, image], "par": [image_par, image_par], "out": [image_out, image_out]},
        "est": estimate,
        "oriented": False,
    }
    got = stage(env, [(0, count, None)], range(-2, 4), (0, 1), store=True)
    est_a, image_a, held = got["est_new"], got["image_new"], got["ratio_new"]
    par_a = to_pair(image_a)
    env["ratio"] = [(held, 0, 6)]
    carry, start, parts = None, 0, []
    for i, size in enumerate(sizes):
        last = start + size == count
        parts.append((start, size, data_out[i]))
        got = stage(env, parts[-1:], (4, 5), (2, 3), last=last, carry=carry)
        carry = None if last else got["sum"]
        start += size
    est_b, image_b = got["est_new"], got["image_new"]

    out_b = to_outer(image_b)
    par_b = to_pair(image_b)
    env.update(
        image={"own": [image_a, image_b], "par": [par_a, par_b], "out": [None, out_b]},
        est=est_a,
        oriented=True,
    )
    near = stage(env, [(0, count, None)], range(-2, 2), (), store=True)["ratio_new"]
    env["image"]["out"][0] = to_outer(after(image_a, near))
    if steps:
        totals = after(totals, near)
        other = fold(totals, steps[-1])
    else:
        totals = lax.psum(totals, "strip")
        other = jnp.zeros_like(totals)
    env["ratio"] = [(near, 0, 4)]
    got = stage(env, [(0, count, None)], (2, 3), (0, 1), store=True)
    middle = got["ratio_new"]
    env["totals"] = (totals, other)
    env["ratio"] = [(near, 0, 4), (middle, 4, 2)]
    env.update(est=est_b, other=got["est_new"])
    return stage(env, parts, (4, 5), (2, 3), final=True)["done"]


def solution(mesh):
    placed = (
        P(("blocks", "strip"), None, None),
        P(None, ("blocks", "strip"), None, None),
        P(),
        P(),
        P(),
    )

    return jax.shard_map(
        local,
        mesh=mesh,
        in_specs=placed,
        out_specs=P(("blocks", "strip"), None, None),
        check_vma=False,
    )
```

```python
import jax
import jax.numpy as jnp
from jax import lax
from jax.experimental import pallas as pl
from jax.experimental.pallas import tpu as pltpu
from jax.sharding import PartitionSpec as P


BF = jnp.bfloat16
F32 = jnp.float32
CHUNKS = (6, 2)
GROUP = 2
GRANT = 6 * 1024 * 1024
FULL = 60 * 1024 * 1024


def dot(left, right):
    return jnp.dot(left, right, preferred_element_type=F32)


def call(body, refs, outs, scratch, work=0, grant=GRANT):
    spaces = {"vmem": pltpu.VMEM, "smem": pltpu.SMEM, "hbm": pltpu.HBM, "any": pl.ANY}
    specs = [pl.BlockSpec(memory_space=spaces[where]) for _, where in refs.values()]
    moved = sum(value.size * value.dtype.itemsize for value, _ in refs.values())

    def kernel(*given):
        names = list(refs) + list(outs)
        body(dict(zip(names, given)), given[len(names) :])

    got = pl.pallas_call(
        kernel,
        in_specs=specs,
        out_specs=[pl.BlockSpec(memory_space=spaces[(*out, "vmem")[2]]) for out in outs.values()],
        out_shape=[jax.ShapeDtypeStruct(*out[:2]) for out in outs.values()],
        scratch_shapes=scratch,
        compiler_params=pltpu.CompilerParams(vmem_limit_bytes=grant),
        cost_estimate=pl.CostEstimate(flops=work, bytes_accessed=moved, transcendentals=0),
    )(*[value for value, _ in refs.values()])
    return dict(zip(outs, got))


def orient(odd, estimate):
    own, nx, nz = estimate.shape

    def body(ref, scratch):
        is_odd = ref["odd"][0]
        for q in range(own):
            ref["image"][q] = ref["est"][is_odd * q + (1 - is_odd) * (own - 1 - q)].astype(BF)

    refs = {"odd": (odd, "smem"), "est": (estimate, "vmem")}
    return call(body, refs, {"image": ((own, nx, nz), BF)}, [])["image"]


def parcel(odd, views, sizes):
    count, own, nx, nz = views.shape
    half = own // 2
    outs = {"a": ((count, half, nx, nz), BF)}
    outs.update({f"b{i}": ((size, half, nx, nz), BF) for i, size in enumerate(sizes)})

    def body(ref, scratch):
        is_odd = ref["odd"][0]
        sems = scratch[0]
        near, far = (1 - is_odd) * half, is_odd * half
        copies = []
        at = 0
        for i, size in enumerate(sizes):
            source = ref["views"].at[pl.ds(at, size), pl.ds(far, half)]
            copies.append(pltpu.make_async_copy(source, ref[f"b{i}"], sems.at[i]))
            at += size
        source = ref["views"].at[:, pl.ds(near, half)]
        copies.append(pltpu.make_async_copy(source, ref["a"], sems.at[len(sizes)]))
        for copy in copies:
            copy.start()
        for copy in copies:
            copy.wait()

    refs = {"odd": (odd, "smem"), "views": (views, "hbm")}
    got = call(body, refs, outs, [pltpu.SemaphoreType.DMA((len(sizes) + 1,))], grant=FULL)
    return got["a"], [got[f"b{i}"] for i in range(len(sizes))]


def sums(views):
    count, own, nx, nz = views.shape

    def body(ref, scratch):
        def step(view, _):
            total = jnp.zeros((8, nz), F32)
            for row in range(own):
                part = ref["views"][view, row].astype(F32)
                total = total + jnp.sum(part.reshape(nx // 8, 8, nz), axis=0)
            total = jnp.sum(jnp.sum(total, axis=0, keepdims=True), axis=1, keepdims=True)
            ref["total"][pl.ds(view, 1), :] = jnp.broadcast_to(total, (1, 128))
            return 0

        lax.fori_loop(0, count, step, 0)

    return call(body, {"views": (views, "vmem")}, {"total": ((count, 128), F32)}, [], grant=FULL)["total"]


def locate_image(p, own):
    if p < 0:
        key, q = "par", -1 - p
    elif p >= own:
        key, q = "out", 2 * own - 1 - p
    else:
        key, q = "own", p
    return key, q


def stage(env, chunks, forward, backward, last=True, carry=None, store=False, final=False):
    views, norm, mats = env["views"], env["norm"], env["mats"]
    count, own, nx, nz = views.shape
    taps = norm.shape[1]
    ry = taps // 2
    half = own // 2
    refs = {"odd": (env["odd"], "smem"), "norm": (norm, "smem"), "mats": (mats, "vmem")}
    reach = {locate_image(p + t - ry, own) for p in forward for t in range(taps)}
    for key, q in sorted(reach):
        value = env["image"][key][q // half]
        refs[f"image_{key}{q // half}"] = (value, "vmem")
    if any(p < 0 for p in forward):
        refs["data_par"] = (env["data_par"], "vmem")
    if any(0 <= p < own for p in forward):
        refs["views"] = (views, "vmem")
    for i, (_, _, data) in enumerate(chunks):
        if data is not None:
            refs[f"data_out{i}"] = (data, "vmem")
    new = [p + ry for p in forward]
    old = sorted({y + t for y in backward for t in range(taps)} - set(new))
    placed = {}
    for k, (value, base, rows) in enumerate(env["ratio"] if old else ()):
        for at in old:
            if base <= at < base + rows:
                refs[f"ratio{k}"] = (value, "vmem")
                placed[at] = (f"ratio{k}", at - base)
    if backward and last:
        for k in sorted({y // half for y in backward}):
            refs[f"est{k}"] = (env["est"][k], "vmem")
        if env["joined"] is not None:
            refs["joined"] = (env["joined"], "vmem")
    if carry is not None:
        refs["carry"] = (carry, "vmem")
    if final:
        refs["total_own"] = (env["totals"][0], "vmem")
        refs["total_other"] = (env["totals"][1], "vmem")
    outs = {}
    if backward and not last:
        outs["sum"] = ((len(backward), nx, nz), F32)
    elif backward and final:
        outs["done"] = ((own, nx, nz), F32)
    elif backward:
        outs["est_new"] = ((half, nx, nz), F32)
        outs["image_new"] = ((half, nx, nz), BF)
        if env["joined"] is not None:
            outs["image_all"] = ((own, nx, nz), BF)
    if store:
        outs["ratio_new"] = ((count, len(new), nx, nz), BF)
    scratch = []
    if backward and last:
        scratch.append(pltpu.VMEM((len(backward), nx, nz), F32))
    if not store:
        scratch.append(pltpu.VMEM((GROUP, len(new), nx, nz), BF))

    def body(ref, scratch):
        is_odd = ref["odd"][0]
        fresh = ref["ratio_new"] if store else scratch[-1]
        total = None
        if backward:
            total = scratch[0] if last else ref["sum"]
            total[...] = ref["carry"][...] if carry is not None else jnp.zeros_like(total)

        def side(q):
            return is_odd * q + (1 - is_odd) * (own - 1 - q)

        def image(p):
            key, q = locate_image(p, own)
            held = ref[f"image_{key}{q // half}"]
            return held[q % half] if held.shape[0] == half else held[q]

        def blur(firsts, along_x, along_z):
            seconds = [dot(along_x, first).astype(BF) for first in firsts]
            result = dot(jnp.concatenate(seconds, axis=0), along_z)
            return [result[i * nx : (i + 1) * nx] for i in range(len(firsts))]

        for i, (start, size, _) in enumerate(chunks):

            def group(members, i=i, start=start):
                def recorded(view, p):
                    if p < 0:
                        q = -1 - p
                        return ref["data_par"][view, is_odd * (half - 1 - q) + (1 - is_odd) * q]
                    if p >= own:
                        q = 2 * own - 1 - p
                        return ref[f"data_out{i}"][view - start, is_odd * (own - 1 - q) + (1 - is_odd) * (q - half)]
                    return ref["views"][view, side(p)]

                def ratio(view, slot, row):
                    if row in new:
                        return fresh[slot, new.index(row)]
                    key, index = placed[row]
                    return ref[key][view, index]

                weights = []
                for view in members:
                    mine = []
                    for t in range(taps):
                        value = ref["norm"][view, is_odd * t + (1 - is_odd) * (taps - 1 - t)]
                        mine.append(jnp.full((nx, nz), value, F32).astype(BF))
                    weights.append(mine)

                def combine(mine, rows):
                    acc = None
                    for weight, row in zip(mine, rows):
                        term = weight * row
                        acc = term if acc is None else acc + term
                    return acc

                slots = [view if store else k for k, view in enumerate(members)]
                for mine, slot, view in zip(weights, slots, members):
                    firsts = [combine(mine, [image(p + t - ry) for t in range(taps)]) for p in forward]
                    for p, blurred in zip(forward, blur(firsts, ref["mats"][view, 0], ref["mats"][view, 1])):
                        fresh[slot, new.index(p + ry)] = (recorded(view, p).astype(F32) / blurred).astype(BF)
                if not backward:
                    return
                product = [None] * len(backward)
                for mine, slot, view in zip(weights, slots, members):
                    firsts = [combine(mine, [ratio(view, slot, y + taps - 1 - t) for t in range(taps)]) for y in backward]
                    for j, value in enumerate(blur(firsts, ref["mats"][view, 2], ref["mats"][view, 3])):
                        product[j] = value if product[j] is None else product[j] * value
                for j, value in enumerate(product):
                    total[j] += jnp.log(value)

            def step(k, _, start=start):
                group([start + GROUP * k + m for m in range(GROUP)])
                return 0

            lax.fori_loop(0, size // GROUP, step, 0)
            for view in range(start + size // GROUP * GROUP, start + size):
                group([view])
        if not (backward and last):
            return
        if final:
            sums_all = ref["total_own"][...] + ref["total_other"][...]
            shares = jnp.sum(sums_all, axis=0, keepdims=True) / (count * sums_all)
            gain = jnp.sum(jnp.log(shares), axis=0, keepdims=True) / count
            gain = jnp.concatenate([gain] * (nz // 128), axis=1)
        for j, y in enumerate(backward):
            value = total[j] / count
            held = ref[f"est{y // half}"]
            if final:
                ref["done"][side(y)] = held[y % half] * jnp.exp(value + gain)
            else:
                value = held[side(y)] * jnp.exp(value)
                ref["est_new"][j] = value
                ref["image_new"][j] = value.astype(BF)
                if "joined" in ref:
                    ref["image_all"][y] = value.astype(BF)
                    ref["image_all"][j] = ref["joined"][j]

    amount = sum(size for _, size, _ in chunks)
    work = 4 * nx * nz * nx * amount * (len(forward) + len(backward))
    return call(body, refs, outs, scratch, work)


def matrices(px, pz, length):
    count, taps = px.shape
    radius = taps // 2

    def body(ref, scratch):
        rows = lax.broadcasted_iota(jnp.int32, (length, length), 0)
        columns = lax.broadcasted_iota(jnp.int32, (length, length), 1)
        for flip in (False, True):
            grid = (columns - rows if flip else rows - columns) + radius
            for key, slot in (("x", 0 if flip else 2), ("z", 3 if flip else 1)):

                def step(view, _, grid=grid, key=key, slot=slot):
                    matrix = jnp.zeros((length, length), F32)
                    for offset in range(taps):
                        matrix = jnp.where(grid == offset, ref[key][view, offset], matrix)
                    ref["mats"][view, slot] = matrix.astype(BF)
                    return 0

                lax.fori_loop(0, count, step, 0)

    refs = {"x": (px, "smem"), "z": (pz, "smem")}
    return call(body, refs, {"mats": ((count, 4, length, length), BF)}, [])["mats"]


def rescaled(norm):
    factors = jnp.exp2(jnp.arange(128, dtype=F32) / 128)
    tried = norm[:, :, None] * factors
    off = lax.reduce_precision(tried, 8, 7) - tried
    cost = jnp.sum(off * off, axis=1) / (factors * factors)
    best = jnp.argmin(cost, axis=1)
    return norm * jnp.exp2(best.astype(F32) / 128)[:, None]


def after(value, other):
    return lax.optimization_barrier((value, other))[0]


def local(estimate, views_data, kernel_x, kernel_y, kernel_z):
    count = views_data.shape[0]
    _, nx, _ = estimate.shape
    strip = lax.axis_size("strip")
    odd = (lax.axis_index("strip") % 2).astype(jnp.int32).reshape(1)
    pair = [(i, i ^ 1) for i in range(strip) if (i ^ 1) < strip]
    outer = []
    for i in range(1, strip - 1, 2):
        outer += [(i, i + 1), (i + 1, i)]

    def to_pair(x):
        return lax.ppermute(x, "strip", pair)

    def to_outer(x):
        return lax.ppermute(x, "strip", outer)

    sizes = list(CHUNKS) if sum(CHUNKS) == count else [1] * count
    image = orient(odd, estimate)
    image_out = to_outer(image)
    image_par = to_pair(image)
    send_a, send_b = parcel(odd, views_data, sizes)
    data_out = [to_outer(b) for b in send_b]
    data_par = to_pair(send_a)

    totals = sums(views_data)
    steps = []
    if strip > 1 and strip & (strip - 1) == 0:
        steps = [1 << k for k in range(strip.bit_length() - 1)]
        steps = [1] + [s for s in steps if s > 2] + [s for s in steps if s == 2]

    def fold(value, step):
        return lax.ppermute(value, "strip", [(i, i ^ step) for i in range(strip)])

    norm = rescaled(kernel_y / jnp.sum(kernel_y, axis=1, keepdims=True))
    px = kernel_x / jnp.sum(kernel_x, axis=1, keepdims=True)
    pz = kernel_z / jnp.sum(kernel_z, axis=1, keepdims=True)
    px, pz, norm, totals = lax.optimization_barrier((px, pz, norm, totals))
    mats = matrices(px, pz, nx)
    totals = after(totals, mats)
    for step in steps[:-1]:
        totals = totals + fold(totals, step)
    norm = after(norm, totals)
    env = {
        "odd": odd,
        "norm": norm,
        "mats": mats,
        "views": views_data,
        "data_par": data_par,
        "image": {"own": [image, image], "par": [image_par, image_par], "out": [image_out, image_out]},
        "est": [estimate, estimate],
        "joined": None,
    }
    got = stage(env, [(0, count, None)], range(-2, 4), (0, 1), store=True)
    est_a, image_a, held = got["est_new"], got["image_new"], got["ratio_new"]
    par_a = to_pair(image_a)
    env["ratio"] = [(held, 0, 6)]
    par_a = to_pair(image_a)
    carry, start, parts = None, 0, []
    for i, size in enumerate(sizes):
        last = start + size == count
        parts.append((start, size, data_out[i]))
        env["joined"] = image_a if last else None
        got = stage(env, parts[-1:], (4, 5), (2, 3), last=last, carry=carry)
        carry = None if last else got["sum"]
        start += size
    est_b, image_b, image_all = got["est_new"], got["image_new"], got["image_all"]

    image_out = to_outer(image_all)
    par_b = to_pair(image_b)
    env.update(
        image={"own": [image_a, image_b], "par": [par_a, par_b], "out": [image_out, image_out]},
        est=[est_a, est_b],
        joined=None,
    )
    near = stage(env, [(0, count, None)], range(-2, 2), (), store=True)["ratio_new"]
    if steps:
        other = fold(after(totals, image_b), steps[-1])
    else:
        totals = lax.psum(totals, "strip")
        other = jnp.zeros_like(totals)
    env["totals"] = (totals, other)
    env["ratio"] = [(near, 0, 4)]
    return stage(env, parts, range(2, 6), range(0, 4), final=True)["done"]


def solution(mesh):
    placed = (
        P(("blocks", "strip"), None, None),
        P(None, ("blocks", "strip"), None, None),
        P(),
        P(),
        P(),
    )

    return jax.shard_map(
        local,
        mesh=mesh,
        in_specs=placed,
        out_specs=P(("blocks", "strip"), None, None),
        check_vma=False,
    )
```

```python
import jax
import jax.numpy as jnp
from jax import lax
from jax.experimental import pallas as pl
from jax.experimental.pallas import tpu as pltpu
from jax.sharding import PartitionSpec as P


BF = jnp.bfloat16
F32 = jnp.float32
VMEM, SMEM, HBM = pltpu.VMEM, pltpu.SMEM, pltpu.HBM
STRIP = "strip"
CHUNKS = (6, 2)
GROUPS = {"near": 4, "far": 3}
GRANT = 6 * 1024 * 1024
FULL = 60 * 1024 * 1024


def dot(left, right):
    return jnp.dot(left, right, preferred_element_type=F32)


def call(body, refs, outs, scratch, work=0, grant=GRANT):
    specs = [pl.BlockSpec(memory_space=where) for _, where in refs.values()]
    moved = sum(value.size * value.dtype.itemsize for value, _ in refs.values())

    def kernel(*given):
        names = list(refs) + list(outs)
        body(dict(zip(names, given)), given[len(names) :])

    got = pl.pallas_call(
        kernel,
        in_specs=specs,
        out_specs=[pl.BlockSpec(memory_space=VMEM) for _ in outs],
        out_shape=[jax.ShapeDtypeStruct(shape, dtype) for shape, dtype in outs.values()],
        scratch_shapes=scratch,
        compiler_params=pltpu.CompilerParams(vmem_limit_bytes=grant),
        cost_estimate=pl.CostEstimate(flops=work, bytes_accessed=moved, transcendentals=0),
    )(*[value for value, _ in refs.values()])
    return dict(zip(outs, got))


def orient(odd, estimate):
    own, nx, nz = estimate.shape

    def body(ref, scratch):
        is_odd = ref["odd"][0]
        for q in range(own):
            ref["image"][q] = ref["est"][is_odd * q + (1 - is_odd) * (own - 1 - q)].astype(BF)

    refs = {"odd": (odd, SMEM), "est": (estimate, VMEM)}
    return call(body, refs, {"image": ((own, nx, nz), BF)}, [])["image"]


def parcel(odd, views, sizes):
    count, own, nx, nz = views.shape
    half = own // 2
    outs = {"a": ((count, half, nx, nz), BF)}
    outs.update({f"b{i}": ((size, half, nx, nz), BF) for i, size in enumerate(sizes)})

    def body(ref, scratch):
        is_odd = ref["odd"][0]
        sems = scratch[0]
        near, far = (1 - is_odd) * half, is_odd * half
        copies = []
        at = 0
        for i, size in enumerate(sizes):
            source = ref["views"].at[pl.ds(at, size), pl.ds(far, half)]
            copies.append(pltpu.make_async_copy(source, ref[f"b{i}"], sems.at[i]))
            at += size
        source = ref["views"].at[:, pl.ds(near, half)]
        copies.append(pltpu.make_async_copy(source, ref["a"], sems.at[len(sizes)]))
        for copy in copies:
            copy.start()
        for copy in copies:
            copy.wait()

    refs = {"odd": (odd, SMEM), "views": (views, HBM)}
    got = call(body, refs, outs, [pltpu.SemaphoreType.DMA((len(sizes) + 1,))], grant=FULL)
    return got["a"], [got[f"b{i}"] for i in range(len(sizes))]


def sums(views):
    count, own, nx, nz = views.shape

    def body(ref, scratch):
        def step(view, _):
            total = jnp.zeros((8, nz), F32)
            for row in range(own):
                part = ref["views"][view, row].astype(F32)
                total = total + jnp.sum(part.reshape(nx // 8, 8, nz), axis=0)
            total = jnp.sum(jnp.sum(total, axis=0, keepdims=True), axis=1, keepdims=True)
            ref["total"][pl.ds(view, 1), :] = jnp.broadcast_to(total, (1, 128))
            return 0

        lax.fori_loop(0, count, step, 0)

    return call(body, {"views": (views, VMEM)}, {"total": ((count, 128), F32)}, [], grant=FULL)["total"]


def locate_image(p, own):
    if p < 0:
        key, q = "par", -1 - p
    elif p >= own:
        key, q = "out", 2 * own - 1 - p
    else:
        key, q = "own", p
    return key, q


def stage(name, env, chunks, forward, backward, last=True, carry=None, store=False, final=False):
    views, norm, mats = env["views"], env["norm"], env["mats"]
    count, own, nx, nz = views.shape
    taps = norm.shape[1]
    ry = taps // 2
    half = own // 2
    group_size = GROUPS.get(name, 2)
    refs = {"odd": (env["odd"], SMEM), "norm": (norm, SMEM), "mats": (mats, VMEM)}
    reach = {locate_image(p + t - ry, own) for p in forward for t in range(taps)}
    for key, q in sorted(reach):
        value = env["image"][key][q // half]
        refs[f"image_{key}{q // half}"] = (value, VMEM)
    if any(p < 0 for p in forward):
        refs["dpar"] = (env["dpar"], VMEM)
    if any(0 <= p < own for p in forward):
        refs["views"] = (views, VMEM)
    for i, (_, _, data) in enumerate(chunks):
        if data is not None:
            refs[f"dout{i}"] = (data, VMEM)
    new = [p + ry for p in forward]
    old = sorted({y + t for y in backward for t in range(taps)} - set(new))
    placed = {}
    for k, (value, base, rows) in enumerate(env["ratio"] if old else ()):
        for at in old:
            if base <= at < base + rows:
                refs[f"ratio{k}"] = (value, VMEM)
                placed[at] = (f"ratio{k}", at - base)
    if backward and last:
        for k in sorted({y // half for y in backward}):
            refs[f"est{k}"] = (env["est"][k], VMEM)
        if env["joined"] is not None:
            refs["joined"] = (env["joined"], VMEM)
    if carry is not None:
        refs["carry"] = (carry, VMEM)
    if final:
        refs["tot0"] = (env["totals"][0], VMEM)
        refs["tot1"] = (env["totals"][1], VMEM)
    outs = {}
    if backward and not last:
        outs["sum"] = ((len(backward), nx, nz), F32)
    elif backward and final:
        outs["done"] = ((own, nx, nz), F32)
    elif backward:
        outs["enew"] = ((half, nx, nz), F32)
        outs["inew"] = ((half, nx, nz), BF)
        if env["joined"] is not None:
            outs["iall"] = ((own, nx, nz), BF)
    if store:
        outs["rnew"] = ((count, len(new), nx, nz), BF)
    scratch = []
    if backward and last:
        scratch.append(pltpu.VMEM((len(backward), nx, nz), F32))
    if not store:
        scratch.append(pltpu.VMEM((group_size, len(new), nx, nz), BF))

    def body(ref, scratch):
        is_odd = ref["odd"][0]
        fresh = ref["rnew"] if store else scratch[-1]
        total = None
        if backward:
            total = scratch[0] if last else ref["sum"]
            total[...] = ref["carry"][...] if carry is not None else jnp.zeros_like(total)

        def side(q):
            return is_odd * q + (1 - is_odd) * (own - 1 - q)

        def image(p):
            key, q = locate_image(p, own)
            held = ref[f"image_{key}{q // half}"]
            return held[q % half] if held.shape[0] == half else held[q]

        def blur(firsts, along_x, along_z):
            seconds = [dot(along_x, first).astype(BF) for first in firsts]
            result = dot(jnp.concatenate(seconds, axis=0), along_z)
            return [result[i * nx : (i + 1) * nx] for i in range(len(firsts))]

        for i, (start, size, _) in enumerate(chunks):

            def group(members, i=i, start=start):
                def recorded(view, p):
                    if p < 0:
                        q = -1 - p
                        return ref["dpar"][view, is_odd * (half - 1 - q) + (1 - is_odd) * q]
                    if p >= own:
                        q = 2 * own - 1 - p
                        return ref[f"dout{i}"][view - start, is_odd * (own - 1 - q) + (1 - is_odd) * (q - half)]
                    return ref["views"][view, side(p)]

                def ratio(view, slot, row):
                    if row in new:
                        return fresh[slot, new.index(row)]
                    key, index = placed[row]
                    return ref[key][view, index]

                weights = []
                for view in members:
                    mine = []
                    for t in range(taps):
                        value = ref["norm"][view, is_odd * t + (1 - is_odd) * (taps - 1 - t)]
                        mine.append(jnp.full((nx, nz), value, F32).astype(BF))
                    weights.append(mine)

                def combine(mine, rows):
                    acc = None
                    for weight, row in zip(mine, rows):
                        term = weight * row
                        acc = term if acc is None else acc + term
                    return acc

                slots = [view if store else k for k, view in enumerate(members)]
                for mine, slot, view in zip(weights, slots, members):
                    firsts = [combine(mine, [image(p + t - ry) for t in range(taps)]) for p in forward]
                    for p, blurred in zip(forward, blur(firsts, ref["mats"][view, 0], ref["mats"][view, 1])):
                        fresh[slot, new.index(p + ry)] = (recorded(view, p).astype(F32) / blurred).astype(BF)
                if not backward:
                    return
                product = [None] * len(backward)
                for k, (mine, slot, view) in enumerate(zip(weights, slots, members)):
                    firsts = [combine(mine, [ratio(view, slot, y + taps - 1 - t) for t in range(taps)]) for y in backward]
                    for j, value in enumerate(blur(firsts, ref["mats"][view, 2], ref["mats"][view, 3])):
                        product[j] = value if k % 2 == 0 else product[j] * value
                    if k % 2 or k + 1 == len(members):
                        for j, value in enumerate(product):
                            total[j] += jnp.log(value)

            def step(k, _, start=start):
                group([start + group_size * k + m for m in range(group_size)])
                return 0

            whole = size // group_size
            if whole > 1:
                lax.fori_loop(0, whole, step, 0)
            elif whole:
                step(0, 0)
            if size % group_size:
                group(list(range(start + whole * group_size, start + size)))
        if not (backward and last):
            return
        if final:
            sums_all = ref["tot0"][...] + ref["tot1"][...]
            shares = jnp.sum(sums_all, axis=0, keepdims=True) / (count * sums_all)
            gain = jnp.sum(jnp.log(shares), axis=0, keepdims=True) / count
            gain = jnp.concatenate([gain] * (nz // 128), axis=1)
        for j, y in enumerate(backward):
            value = total[j] / count
            held = ref[f"est{y // half}"]
            if final:
                ref["done"][side(y)] = held[y % half] * jnp.exp(value + gain)
            else:
                value = held[side(y)] * jnp.exp(value)
                ref["enew"][j] = value
                ref["inew"][j] = value.astype(BF)
                if "joined" in ref:
                    ref["iall"][y] = value.astype(BF)
                    ref["iall"][j] = ref["joined"][j]

    amount = sum(size for _, size, _ in chunks)
    work = 4 * nx * nz * nx * amount * (len(forward) + len(backward))
    return call(body, refs, outs, scratch, work)


def matrices(px, pz, length):
    count, taps = px.shape
    radius = taps // 2

    def body(ref, scratch):
        rows = lax.broadcasted_iota(jnp.int32, (length, length), 0)
        columns = lax.broadcasted_iota(jnp.int32, (length, length), 1)
        for flip in (False, True):
            grid = (columns - rows if flip else rows - columns) + radius
            for key, slot in (("x", 0 if flip else 2), ("z", 3 if flip else 1)):

                def step(view, _, grid=grid, key=key, slot=slot):
                    matrix = jnp.zeros((length, length), F32)
                    for offset in range(taps):
                        matrix = jnp.where(grid == offset, ref[key][view, offset], matrix)
                    ref["mats"][view, slot] = matrix.astype(BF)
                    return 0

                lax.fori_loop(0, count, step, 0)

    refs = {"x": (px, SMEM), "z": (pz, SMEM)}
    return call(body, refs, {"mats": ((count, 4, length, length), BF)}, [])["mats"]


def rescaled(norm):
    factors = jnp.exp2(jnp.arange(128, dtype=F32) / 128)
    tried = norm[:, :, None] * factors
    off = lax.reduce_precision(tried, 8, 7) - tried
    cost = jnp.sum(off * off, axis=1) / (factors * factors)
    best = jnp.argmin(cost, axis=1)
    return norm * jnp.exp2(best.astype(F32) / 128)[:, None]


def after(value, other):
    return lax.optimization_barrier((value, other))[0]


def local(estimate, views_data, kernel_x, kernel_y, kernel_z):
    count = views_data.shape[0]
    _, nx, _ = estimate.shape
    strip = lax.axis_size(STRIP)
    odd = (lax.axis_index(STRIP) % 2).astype(jnp.int32).reshape(1)
    pair = [(i, i ^ 1) for i in range(strip) if (i ^ 1) < strip]
    outer = []
    for i in range(1, strip - 1, 2):
        outer += [(i, i + 1), (i + 1, i)]

    def to_pair(x):
        return lax.ppermute(x, STRIP, pair)

    def to_outer(x):
        return lax.ppermute(x, STRIP, outer)

    sizes = list(CHUNKS) if sum(CHUNKS) == count else [1] * count
    image = orient(odd, estimate)
    image_out = to_outer(image)
    image_par = to_pair(image)
    send_a, send_b = parcel(odd, views_data, sizes)
    data_out = [to_outer(b) for b in send_b]
    data_par = to_pair(send_a)

    totals = sums(views_data)
    steps = []
    if strip > 1 and strip & (strip - 1) == 0:
        steps = [1 << k for k in range(strip.bit_length() - 1)]
        steps = [1] + [s for s in steps if s > 2] + [s for s in steps if s == 2]

    def fold(value, step):
        return lax.ppermute(value, STRIP, [(i, i ^ step) for i in range(strip)])

    norm = rescaled(kernel_y / jnp.sum(kernel_y, axis=1, keepdims=True))
    px = kernel_x / jnp.sum(kernel_x, axis=1, keepdims=True)
    pz = kernel_z / jnp.sum(kernel_z, axis=1, keepdims=True)
    px, pz, norm, totals = lax.optimization_barrier((px, pz, norm, totals))
    mats = matrices(px, pz, nx)
    totals = after(totals, mats)
    for step in steps[:-1]:
        totals = totals + fold(totals, step)
    norm = after(norm, totals)
    env = {
        "odd": odd,
        "norm": norm,
        "mats": mats,
        "views": views_data,
        "dpar": data_par,
        "image": {"own": [image, image], "par": [image_par, image_par], "out": [image_out, image_out]},
        "est": [estimate, estimate],
        "joined": None,
    }
    got = stage("inner", env, [(0, count, None)], range(-2, 4), (0, 1), store=True)
    est_a, image_a, held = got["enew"], got["inew"], got["rnew"]
    par_a = to_pair(image_a)
    env["ratio"] = [(held, 0, 6)]
    par_a = to_pair(image_a)
    carry, start, parts = None, 0, []
    for i, size in enumerate(sizes):
        last = start + size == count
        parts.append((start, size, data_out[i]))
        env["joined"] = image_a if last else None
        got = stage("outer", env, parts[-1:], (4, 5), (2, 3), last=last, carry=carry)
        carry = None if last else got["sum"]
        start += size
    est_b, image_b, image_all = got["enew"], got["inew"], got["iall"]

    image_out = to_outer(image_all)
    par_b = to_pair(image_b)
    env.update(
        image={"own": [image_a, image_b], "par": [par_a, par_b], "out": [image_out, image_out]},
        est=[est_a, est_b],
        joined=None,
    )
    near = stage("near", env, [(0, count, None)], range(-2, 2), (), store=True)["rnew"]
    if steps:
        other = fold(after(totals, image_b), steps[-1])
    else:
        totals = lax.psum(totals, STRIP)
        other = jnp.zeros_like(totals)
    env["totals"] = (totals, other)
    env["ratio"] = [(near, 0, 4)]
    return stage("far", env, parts, range(2, 6), range(0, 4), final=True)["done"]


def solution(mesh):
    placed = (
        P(("blocks", STRIP), None, None),
        P(None, ("blocks", STRIP), None, None),
        P(),
        P(),
        P(),
    )

    return jax.shard_map(
        local,
        mesh=mesh,
        in_specs=placed,
        out_specs=P(("blocks", STRIP), None, None),
        check_vma=False,
    )
```

```python
import jax
import jax.numpy as jnp
from jax import lax
from jax.experimental import pallas as pl
from jax.experimental.pallas import tpu as pltpu
from jax.sharding import PartitionSpec as P


BF = jnp.bfloat16
F32 = jnp.float32
VMEM, SMEM, HBM = pltpu.VMEM, pltpu.SMEM, pltpu.HBM
STRIP = "strip"
CHUNKS = (6, 2)
GROUPS = {"near": 4, "far": 6}
GRANT = 6 * 1024 * 1024
FULL = 60 * 1024 * 1024


def dot(left, right):
    return jnp.dot(left, right, preferred_element_type=F32)


def call(body, refs, outs, scratch, work=0, grant=GRANT):
    specs = [pl.BlockSpec(memory_space=where) for _, where in refs.values()]
    moved = sum(value.size * value.dtype.itemsize for value, _ in refs.values())

    def kernel(*given):
        names = list(refs) + list(outs)
        body(dict(zip(names, given)), given[len(names) :])

    got = pl.pallas_call(
        kernel,
        in_specs=specs,
        out_specs=[pl.BlockSpec(memory_space=(*out, VMEM)[2]) for out in outs.values()],
        out_shape=[jax.ShapeDtypeStruct(*out[:2]) for out in outs.values()],
        scratch_shapes=scratch,
        compiler_params=pltpu.CompilerParams(vmem_limit_bytes=grant),
        cost_estimate=pl.CostEstimate(flops=work, bytes_accessed=moved, transcendentals=0),
    )(*[value for value, _ in refs.values()])
    return dict(zip(outs, got))


def orient(odd, estimate):
    own, nx, nz = estimate.shape

    def body(ref, scratch):
        is_odd = ref["odd"][0]
        for q in range(own):
            ref["image"][q] = ref["est"][is_odd * q + (1 - is_odd) * (own - 1 - q)].astype(BF)

    refs = {"odd": (odd, SMEM), "est": (estimate, VMEM)}
    return call(body, refs, {"image": ((own, nx, nz), BF)}, [])["image"]


def parcel(odd, views, sizes):
    count, own, nx, nz = views.shape
    half = own // 2
    outs = {"a": ((count, half, nx, nz), BF)}
    outs.update({f"b{i}": ((size, half, nx, nz), BF) for i, size in enumerate(sizes)})

    def body(ref, scratch):
        is_odd = ref["odd"][0]
        sems = scratch[0]
        near, far = (1 - is_odd) * half, is_odd * half
        copies = []
        at = 0
        for i, size in enumerate(sizes):
            source = ref["views"].at[pl.ds(at, size), pl.ds(far, half)]
            copies.append(pltpu.make_async_copy(source, ref[f"b{i}"], sems.at[i]))
            at += size
        source = ref["views"].at[:, pl.ds(near, half)]
        copies.append(pltpu.make_async_copy(source, ref["a"], sems.at[len(sizes)]))
        for copy in copies:
            copy.start()
        for copy in copies:
            copy.wait()

    refs = {"odd": (odd, SMEM), "views": (views, HBM)}
    got = call(body, refs, outs, [pltpu.SemaphoreType.DMA((len(sizes) + 1,))], grant=FULL)
    return got["a"], [got[f"b{i}"] for i in range(len(sizes))]


def sums(views):
    count, own, nx, nz = views.shape

    def body(ref, scratch):
        def step(view, _):
            total = jnp.zeros((8, nz), F32)
            for row in range(own):
                part = ref["views"][view, row].astype(F32)
                total = total + jnp.sum(part.reshape(nx // 8, 8, nz), axis=0)
            total = jnp.sum(jnp.sum(total, axis=0, keepdims=True), axis=1, keepdims=True)
            ref["total"][pl.ds(view, 1), :] = jnp.broadcast_to(total, (1, 128))
            return 0

        lax.fori_loop(0, count, step, 0)

    return call(body, {"views": (views, VMEM)}, {"total": ((count, 128), F32)}, [], grant=FULL)["total"]


def locate_image(p, own):
    if p < 0:
        key, q = "par", -1 - p
    elif p >= own:
        key, q = "out", 2 * own - 1 - p
    else:
        key, q = "own", p
    return key, q


def stage(name, env, chunks, forward, backward, last=True, carry=None, store=False, final=False):
    views, norm, mats = env["views"], env["norm"], env["mats"]
    count, own, nx, nz = views.shape
    taps = norm.shape[1]
    ry = taps // 2
    half = own // 2
    group_size = GROUPS.get(name, 2)
    refs = {"odd": (env["odd"], SMEM), "norm": (norm, SMEM), "mats": (mats, VMEM)}
    reach = {locate_image(p + t - ry, own) for p in forward for t in range(taps)}
    for key, q in sorted(reach):
        value = env["image"][key][q // half]
        refs[f"image_{key}{q // half}"] = (value, VMEM)
    if any(p < 0 for p in forward):
        refs["dpar"] = (env["dpar"], VMEM)
    if any(0 <= p < own for p in forward):
        refs["views"] = (views, VMEM)
    for i, (_, _, data) in enumerate(chunks):
        if data is not None:
            refs[f"dout{i}"] = (data, VMEM)
    new = [p + ry for p in forward]
    old = sorted({y + t for y in backward for t in range(taps)} - set(new))
    placed = {}
    for k, (value, base, rows) in enumerate(env["ratio"] if old else ()):
        for at in old:
            if base <= at < base + rows:
                refs[f"ratio{k}"] = (value, VMEM)
                placed[at] = (f"ratio{k}", at - base)
    if backward and last:
        for k in sorted({y // half for y in backward}):
            refs[f"est{k}"] = (env["est"][k], VMEM)
        if env["joined"] is not None:
            refs["joined"] = (env["joined"], VMEM)
    if carry is not None:
        refs["carry"] = (carry, VMEM)
    if final:
        refs["tot0"] = (env["totals"][0], VMEM)
        refs["tot1"] = (env["totals"][1], VMEM)
    outs = {}
    if backward and not last:
        outs["sum"] = ((len(backward), nx, nz), F32)
    elif backward and final:
        outs["done"] = ((own, nx, nz), F32, pl.ANY)
    elif backward:
        outs["enew"] = ((half, nx, nz), F32)
        outs["inew"] = ((half, nx, nz), BF)
        if env["joined"] is not None:
            outs["iall"] = ((own, nx, nz), BF)
    if store:
        outs["rnew"] = ((count, len(new), nx, nz), BF)
    scratch = []
    if backward and last:
        scratch.append(pltpu.VMEM((len(backward), nx, nz), F32))
    if final:
        scratch.insert(0, pltpu.SemaphoreType.DMA((len(backward),)))
    if not store:
        scratch.append(pltpu.VMEM((group_size, len(new), nx, nz), BF))

    def body(ref, scratch):
        is_odd = ref["odd"][0]
        fresh = ref["rnew"] if store else scratch[-1]
        total = None
        if backward:
            total = scratch[1 if final else 0] if last else ref["sum"]
            total[...] = ref["carry"][...] if carry is not None else jnp.zeros_like(total)

        def side(q):
            return is_odd * q + (1 - is_odd) * (own - 1 - q)

        def image(p):
            key, q = locate_image(p, own)
            held = ref[f"image_{key}{q // half}"]
            return held[q % half] if held.shape[0] == half else held[q]

        def blur(firsts, along_x, along_z):
            seconds = [dot(along_x, first).astype(BF) for first in firsts]
            result = dot(jnp.concatenate(seconds, axis=0), along_z)
            return [result[i * nx : (i + 1) * nx] for i in range(len(firsts))]

        for i, (start, size, _) in enumerate(chunks):

            def group(members, i=i, start=start):
                def recorded(view, p):
                    if p < 0:
                        q = -1 - p
                        return ref["dpar"][view, is_odd * (half - 1 - q) + (1 - is_odd) * q]
                    if p >= own:
                        q = 2 * own - 1 - p
                        return ref[f"dout{i}"][view - start, is_odd * (own - 1 - q) + (1 - is_odd) * (q - half)]
                    return ref["views"][view, side(p)]

                def ratio(view, slot, row):
                    if row in new:
                        return fresh[slot, new.index(row)]
                    key, index = placed[row]
                    return ref[key][view, index]

                weights = []
                for view in members:
                    mine = []
                    for t in range(taps):
                        value = ref["norm"][view, is_odd * t + (1 - is_odd) * (taps - 1 - t)]
                        mine.append(jnp.full((nx, nz), value, F32).astype(BF))
                    weights.append(mine)

                def combine(mine, rows):
                    acc = None
                    for weight, row in zip(mine, rows):
                        term = weight * row
                        acc = term if acc is None else acc + term
                    return acc

                slots = [view if store else k for k, view in enumerate(members)]
                for mine, slot, view in zip(weights, slots, members):
                    firsts = [combine(mine, [image(p + t - ry) for t in range(taps)]) for p in forward]
                    for p, blurred in zip(forward, blur(firsts, ref["mats"][view, 0], ref["mats"][view, 1])):
                        fresh[slot, new.index(p + ry)] = (recorded(view, p).astype(F32) / blurred).astype(BF)
                if not backward:
                    return
                product = [None] * len(backward)
                for k, (mine, slot, view) in enumerate(zip(weights, slots, members)):
                    firsts = [combine(mine, [ratio(view, slot, y + taps - 1 - t) for t in range(taps)]) for y in backward]
                    for j, value in enumerate(blur(firsts, ref["mats"][view, 2], ref["mats"][view, 3])):
                        product[j] = value if k % 2 == 0 else product[j] * value
                    if k % 2 or k + 1 == len(members):
                        for j, value in enumerate(product):
                            total[j] += jnp.log(value)

            def step(k, _, start=start):
                group([start + group_size * k + m for m in range(group_size)])
                return 0

            whole = size // group_size
            if whole > 1:
                lax.fori_loop(0, whole, step, 0)
            elif whole:
                step(0, 0)
            if size % group_size:
                group(list(range(start + whole * group_size, start + size)))
        if not (backward and last):
            return
        if final:
            sums_all = ref["tot0"][...] + ref["tot1"][...]
            shares = jnp.sum(sums_all, axis=0, keepdims=True) / (count * sums_all)
            gain = jnp.sum(jnp.log(shares), axis=0, keepdims=True) / count
            gain = jnp.concatenate([gain] * (nz // 128), axis=1)
        copies = []
        for j, y in enumerate(backward):
            value = total[j] / count
            held = ref[f"est{y // half}"]
            if final:
                total[j] = held[y % half] * jnp.exp(value + gain)
                copies.append(pltpu.make_async_copy(total.at[j], ref["done"].at[side(y)], scratch[0].at[j]))
                copies[-1].start()
            else:
                value = held[side(y)] * jnp.exp(value)
                ref["enew"][j] = value
                ref["inew"][j] = value.astype(BF)
                if "joined" in ref:
                    ref["iall"][y] = value.astype(BF)
                    ref["iall"][j] = ref["joined"][j]
        for copy in copies:
            copy.wait()

    amount = sum(size for _, size, _ in chunks)
    work = 4 * nx * nz * nx * amount * (len(forward) + len(backward))
    return call(body, refs, outs, scratch, work)


def matrices(px, pz, length):
    count, taps = px.shape
    radius = taps // 2

    def body(ref, scratch):
        rows = lax.broadcasted_iota(jnp.int32, (length, length), 0)
        columns = lax.broadcasted_iota(jnp.int32, (length, length), 1)
        for flip in (False, True):
            grid = (columns - rows if flip else rows - columns) + radius
            for key, slot in (("x", 0 if flip else 2), ("z", 3 if flip else 1)):

                def step(view, _, grid=grid, key=key, slot=slot):
                    matrix = jnp.zeros((length, length), F32)
                    for offset in range(taps):
                        matrix = jnp.where(grid == offset, ref[key][view, offset], matrix)
                    ref["mats"][view, slot] = matrix.astype(BF)
                    return 0

                lax.fori_loop(0, count, step, 0)

    refs = {"x": (px, SMEM), "z": (pz, SMEM)}
    return call(body, refs, {"mats": ((count, 4, length, length), BF)}, [])["mats"]


def rescaled(norm):
    factors = jnp.exp2(jnp.arange(128, dtype=F32) / 128)
    tried = norm[:, :, None] * factors
    off = lax.reduce_precision(tried, 8, 7) - tried
    cost = jnp.sum(off * off, axis=1) / (factors * factors)
    best = jnp.argmin(cost, axis=1)
    return norm * jnp.exp2(best.astype(F32) / 128)[:, None]


def after(value, other):
    return lax.optimization_barrier((value, other))[0]


def local(estimate, views_data, kernel_x, kernel_y, kernel_z):
    count = views_data.shape[0]
    _, nx, _ = estimate.shape
    strip = lax.axis_size(STRIP)
    odd = (lax.axis_index(STRIP) % 2).astype(jnp.int32).reshape(1)
    pair = [(i, i ^ 1) for i in range(strip) if (i ^ 1) < strip]
    outer = []
    for i in range(1, strip - 1, 2):
        outer += [(i, i + 1), (i + 1, i)]

    def to_pair(x):
        return lax.ppermute(x, STRIP, pair)

    def to_outer(x):
        return lax.ppermute(x, STRIP, outer)

    sizes = list(CHUNKS) if sum(CHUNKS) == count else [1] * count
    image = orient(odd, estimate)
    image_out = to_outer(image)
    image_par = to_pair(image)
    send_a, send_b = parcel(odd, views_data, sizes)
    data_out = [to_outer(b) for b in send_b]
    data_par = to_pair(send_a)

    totals = sums(views_data)
    steps = []
    if strip > 1 and strip & (strip - 1) == 0:
        steps = [1 << k for k in range(strip.bit_length() - 1)]
        steps = [1] + [s for s in steps if s > 2] + [s for s in steps if s == 2]

    def fold(value, step):
        return lax.ppermute(value, STRIP, [(i, i ^ step) for i in range(strip)])

    norm = rescaled(kernel_y / jnp.sum(kernel_y, axis=1, keepdims=True))
    px = kernel_x / jnp.sum(kernel_x, axis=1, keepdims=True)
    pz = kernel_z / jnp.sum(kernel_z, axis=1, keepdims=True)
    px, pz, norm, totals = lax.optimization_barrier((px, pz, norm, totals))
    mats = matrices(px, pz, nx)
    totals = after(totals, mats)
    for step in steps[:-1]:
        totals = totals + fold(totals, step)
    norm = after(norm, totals)
    env = {
        "odd": odd,
        "norm": norm,
        "mats": mats,
        "views": views_data,
        "dpar": data_par,
        "image": {"own": [image, image], "par": [image_par, image_par], "out": [image_out, image_out]},
        "est": [estimate, estimate],
        "joined": None,
    }
    got = stage("inner", env, [(0, count, None)], range(-2, 4), (0, 1), store=True)
    est_a, image_a, held = got["enew"], got["inew"], got["rnew"]
    par_a = to_pair(image_a)
    env["ratio"] = [(held, 0, 6)]
    par_a = to_pair(image_a)
    carry, start, parts = None, 0, []
    for i, size in enumerate(sizes):
        last = start + size == count
        parts.append((start, size, data_out[i]))
        env["joined"] = image_a if last else None
        got = stage("outer", env, parts[-1:], (4, 5), (2, 3), last=last, carry=carry)
        carry = None if last else got["sum"]
        start += size
    est_b, image_b, image_all = got["enew"], got["inew"], got["iall"]

    image_out = to_outer(image_all)
    par_b = to_pair(image_b)
    env.update(
        image={"own": [image_a, image_b], "par": [par_a, par_b], "out": [image_out, image_out]},
        est=[est_a, est_b],
        joined=None,
    )
    near = stage("near", env, [(0, count, None)], range(-2, 2), (), store=True)["rnew"]
    if steps:
        other = fold(after(totals, image_b), steps[-1])
    else:
        totals = lax.psum(totals, STRIP)
        other = jnp.zeros_like(totals)
    env["totals"] = (totals, other)
    env["ratio"] = [(near, 0, 4)]
    return stage("far", env, parts, range(2, 6), range(0, 4), final=True)["done"]


def solution(mesh):
    placed = (
        P(("blocks", STRIP), None, None),
        P(None, ("blocks", STRIP), None, None),
        P(),
        P(),
        P(),
    )

    return jax.shard_map(
        local,
        mesh=mesh,
        in_specs=placed,
        out_specs=P(("blocks", STRIP), None, None),
        check_vma=False,
    )
```
